32 devices in a mesh: groups: 2 (over y), seq: 4 (over z), head: 2 (over x), rep: 2 (over core).
Axes of the slice: x: 2, y: 2, z: 4, core: 2. Of those that a mesh axis runs over, the one named last changes fastest.
Arguments:
- queries: bfloat16 [8192, 5120], P(('groups', 'seq'), ('head', 'rep')), parts along dimension 0, may hold values from -4.5 to 4.5
- keys: bfloat16 [8192, 5120], P(('groups', 'seq'), ('head', 'rep')), parts along dimension 0, may hold values from -4.5 to 4.5
- values: bfloat16 [8192, 5120], P(('groups', 'seq'), ('head', 'rep')), parts along dimension 0, may hold values from -5 to 5
- rates: float32 [40, 8192], P(('head', 'rep'), ('groups', 'seq')), parts along dimension 1, may hold values from 0.0005 to 0.005
- fast_weights: bfloat16 [128, 40, 3, 128], P(None, ('head', 'rep')), may hold values from -0.5 to 0.5
- momentum: float32 [128, 40, 3, 128], P('seq', ('head', 'rep')), may hold values from -0.3 to 0.3
Outputs:
- mixed: bfloat16 [8192, 5120], P(('groups', 'seq'), ('head', 'rep')), parts along dimension 0
- new_weights: bfloat16 [256, 40, 3, 128], P(('groups', 'seq'), ('head', 'rep')), parts along dimension 0
- new_momentum: float32 [256, 40, 3, 128], P(('groups', 'seq'), ('head', 'rep')), parts along dimension 0
The draws below stay inside these ranges and needn't reach their ends.
There are 2 independent parts, one for each index of `groups`. The reference program is written for one: setup_inputs(seed, part) draws one part's arguments, and reference() takes and returns one part's arrays. A program takes and returns all parts, laid end to end along the dimension named above; an argument that names none is the same for every part. Nothing has to cross between parts.
All inputs are finite; a program needn't handle non-finite values.
Results may differ from the reference program's by a relative error of at most 0.013.
Values may be sent and summed in bfloat16 or wider, within the bound.
No kernel may reach another device: no remote copies, remote signals or barrier semaphores. Data moves between devices by JAX's collectives and lax.ppermute only.
A program may use at most 128 MiB of HBM per device.

```python
import math
import jax
import jax.numpy as jnp
from jax import lax

HEADS = 40
DH = 128
FH = 128
WIN = 512
TOKENS = 4096


def query_key_pair(key):
    base = jax.random.fold_in(key, 7301)
    shape = (TOKENS, HEADS * DH)
    queries = jax.random.truncated_normal(jax.random.fold_in(base, 1), -4.0, 4.0, shape, jnp.float32)
    keys = jax.random.truncated_normal(jax.random.fold_in(base, 2), -4.0, 4.0, shape, jnp.float32)
    return (queries, keys)


def draw_queries(key, part):
    return query_key_pair(key)[0].astype(jnp.bfloat16)


def draw_keys(key, part):
    return query_key_pair(key)[1].astype(jnp.bfloat16)


def block_levels(key, dims, pieces, low, largest):
    level, own = 1.0, jax.random.fold_in(key, 6)
    for position, parts in pieces:
        heights = jnp.exp(jax.random.uniform(jax.random.fold_in(own, position), (parts,), jnp.float32, low / len(pieces), largest / len(pieces)))
        level = level * jnp.repeat(heights, dims[position] // parts).reshape([-1 if axis == position else 1 for axis in range(len(dims))])
    return level


def noise(key, dims, spread, bound, cuts=(), kind=jnp.bfloat16):
    loudness = block_levels(key, dims, cuts, -0.22, 0.18) if cuts else 1.0
    drawn = jax.random.normal(key, dims, jnp.float32) * spread * loudness
    return jnp.minimum(jnp.maximum(drawn, -bound), bound).astype(kind)


def setup_inputs(seed: int = 0, part: int = 0) -> dict:
    streams_of = jax.random.split(jax.random.key(seed), 7)
    part_keys = jax.random.split(jax.random.fold_in(streams_of[6], part), 7)
    return {
        "queries": draw_queries(jax.random.fold_in(jax.random.fold_in(streams_of[6], part), 71), part),
        "keys": draw_keys(jax.random.fold_in(jax.random.fold_in(streams_of[6], part), 71), part),
        "values": noise(part_keys[2], (TOKENS, HEADS * DH), 1.0, 5.0, ((0, 4), (1, 4))),
        "rates": jnp.clip(jnp.exp(math.log(0.005) - 2.30258502 * jax.random.uniform(part_keys[3], (HEADS, TOKENS), jnp.float32) ** block_levels(part_keys[3], (HEADS, TOKENS), ((0, 4), (1, 4)), -0.2, 0.2)), 0.0005, 0.005),
        "fast_weights": noise(streams_of[4], (DH, HEADS, 3, FH), DH ** -0.5, 0.5, ((1, 4),)),
        "momentum": noise(streams_of[5], (DH, HEADS, 3, FH), 0.05, 0.3, ((0, 4), (1, 4)), jnp.float32),
    }


momentum_keep = 0.9
epsilon = 1e-06

def window_block(query_block, key_block, value_block, first):
    width = query_block.shape[0]
    head_size = query_block.shape[2]
    scores = jnp.einsum('qhd,khd->hqk', query_block.astype(jnp.float32), key_block.astype(jnp.float32)) * head_size ** (-0.5)
    query_index = jnp.arange(width, dtype=jnp.int32)[:, None]
    key_index = jnp.arange(2 * width, dtype=jnp.int32)[None, :]
    allowed = (key_index > query_index) & (key_index <= query_index + width) & (key_index + first >= 0)
    scores = jnp.where(allowed[None], scores, -1e+30)
    row_max = lax.optimization_barrier(jnp.max(scores, axis=-1, keepdims=True))
    weights = jnp.exp(scores - row_max)
    total = lax.optimization_barrier(jnp.sum(weights, axis=-1, keepdims=True))
    probabilities = (weights / total).astype(jnp.bfloat16)
    return jnp.einsum('hqk,khd->qhd', probabilities.astype(jnp.float32), value_block.astype(jnp.float32))

def swiglu_parts(inputs, weights):
    inner = jnp.einsum('thr,rhcf->thcf', inputs.astype(jnp.float32), weights[:, :, 0:2].astype(jnp.float32))
    return (inner[:, :, 0], inner[:, :, 1])

def reference(queries, keys, values, rates, fast_weights, momentum):
    query_heads = queries.reshape(TOKENS, HEADS, DH)
    key_heads = keys.reshape(TOKENS, HEADS, DH)
    value_heads = values.reshape(TOKENS, HEADS, DH)
    gating, upward = swiglu_parts(key_heads, fast_weights)
    sigmoid_gate = jax.nn.sigmoid(gating)
    hidden = (gating * sigmoid_gate * upward).astype(jnp.bfloat16)
    scaled_values = (value_heads.astype(jnp.float32) * jnp.transpose(rates)[:, :, None]).astype(jnp.bfloat16)
    hidden_grad = jnp.einsum('thr,rhf->thf', scaled_values.astype(jnp.float32), fast_weights[:, :, 2].astype(jnp.float32))
    gate_grad = (hidden_grad * upward * sigmoid_gate * (1.0 + gating * (1.0 - sigmoid_gate))).astype(jnp.bfloat16)
    upward_grad = (hidden_grad * gating * sigmoid_gate).astype(jnp.bfloat16)
    paired = jnp.stack([gate_grad, upward_grad], axis=2)
    first_grads = jnp.einsum('thr,thcf->rhcf', key_heads.astype(jnp.float32), paired.astype(jnp.float32))
    second_grads = jnp.einsum('thr,thf->rhf', scaled_values.astype(jnp.float32), hidden.astype(jnp.float32))[:, :, None]
    grads = jnp.concatenate([first_grads, second_grads], axis=2)
    new_momentum = momentum_keep * momentum + grads
    before = fast_weights.astype(jnp.float32)
    moved = before + new_momentum
    ratio = jnp.sqrt((lax.optimization_barrier(jnp.mean(before * before, axis=-1, keepdims=True)) + epsilon) / (lax.optimization_barrier(jnp.mean(moved * moved, axis=-1, keepdims=True)) + epsilon))
    new_weights = (moved * ratio).astype(jnp.bfloat16)
    query_gating, query_upward = swiglu_parts(query_heads, new_weights)
    query_hidden = (jax.nn.silu(query_gating) * query_upward).astype(jnp.bfloat16)
    fast_out = jnp.einsum('thf,rhf->thr', query_hidden.astype(jnp.float32), new_weights[:, :, 2].astype(jnp.float32))
    padding = jnp.zeros((WIN, HEADS, DH), jnp.bfloat16)
    padded_keys = jnp.concatenate([padding, key_heads], axis=0)
    padded_values = jnp.concatenate([padding, value_heads], axis=0)

    def one_block(block):
        query_block = lax.dynamic_slice_in_dim(query_heads, block * WIN, WIN, 0)
        key_block = lax.dynamic_slice_in_dim(padded_keys, block * WIN, 2 * WIN, 0)
        value_block = lax.dynamic_slice_in_dim(padded_values, block * WIN, 2 * WIN, 0)
        return window_block(query_block, key_block, value_block, block * WIN - WIN)
    attended = lax.map(one_block, jnp.arange(TOKENS // WIN, dtype=jnp.int32)).reshape(TOKENS, HEADS, DH)
    mixed = (fast_out + attended).reshape(TOKENS, HEADS * DH).astype(jnp.bfloat16)
    return (mixed, new_weights, new_momentum)
```

```python
import functools

import jax
import jax.numpy as jnp
from jax import lax
from jax.experimental import pallas as pl
from jax.experimental.pallas import tpu as pltpu
from jax.sharding import PartitionSpec as P

WIN = 512
TILE = 256

momentum_keep = 0.9
epsilon = 1e-06
MASKED = -1e30
NT = (((1,), (1,)), ((), ()))


def call(body, name, grid, in_specs, out_specs, out_shape, scratch=(), prefetch=0, flops=0, nbytes=0):
    return pl.pallas_call(
        body,
        name=name,
        out_shape=out_shape,
        grid_spec=pltpu.PrefetchScalarGridSpec(
            num_scalar_prefetch=prefetch,
            grid=grid,
            in_specs=in_specs,
            out_specs=out_specs,
            scratch_shapes=list(scratch),
        ),
        cost_estimate=pl.CostEstimate(flops=flops, bytes_accessed=nbytes, transcendentals=0),
    )


def sigmoid(x):
    return 0.5 * jnp.tanh(0.5 * x) + 0.5


def dot(a, b, dims=None):
    if dims is None:
        return jnp.dot(a, b, preferred_element_type=jnp.float32)
    return lax.dot_general(a, b, dims, preferred_element_type=jnp.float32)


def grad_body(peers, z_ref, k_ref, v_ref, r_ref, w_ref, *refs):
    outs, total = refs[:peers], refs[peers]
    size = k_ref.shape[1]
    keys, values = k_ref[...], v_ref[...]
    turned = jnp.transpose(w_ref[...])
    rate = r_ref[pl.ds(pl.program_id(0), 1), :]
    inner = dot(turned[: 2 * size], keys, NT)
    gate, up = inner[:size], inner[size:]
    hidden_grad = dot(turned[2 * size :], values, NT) * rate
    sig = sigmoid(gate)
    silu = gate * sig
    hidden = (silu * up * rate).astype(jnp.bfloat16)
    gate_grad = (hidden_grad * up * (sig + silu * (1.0 - sig))).astype(jnp.bfloat16)
    up_grad = (hidden_grad * silu).astype(jnp.bfloat16)
    total[:, :size] = jnp.transpose(dot(gate_grad, keys))
    total[:, size : 2 * size] = jnp.transpose(dot(up_grad, keys))
    total[:, 2 * size :] = jnp.transpose(dot(hidden, values))
    own = outs[0].shape[0]
    for m in range(peers):
        row = pl.multiple_of((z_ref[0] ^ m) * own, own)
        outs[m][...] = total[pl.ds(row, own), :].astype(outs[m].dtype)


def partial_grads(z, keys, values, rates, weights, peers, kinds):
    rows, heads = keys.shape[0], rates.shape[0]
    size = weights.shape[0]
    own = size // peers
    column = pl.BlockSpec((rows, size), lambda h, z: (0, h))
    return call(
        functools.partial(grad_body, peers),
        "grads",
        (heads,),
        [
            column,
            column,
            pl.BlockSpec((heads, rows), lambda h, z: (0, 0)),
            pl.BlockSpec((size, 3 * size), lambda h, z: (0, h)),
        ],
        [pl.BlockSpec((own, 3 * size), lambda h, z: (0, h))] * peers,
        [jax.ShapeDtypeStruct((own, heads * 3 * size), kind) for kind in kinds],
        [pltpu.VMEM((size, 3 * size), jnp.float32)],
        1,
        12 * rows * heads * size * size,
        4 * rows * heads * size,
    )(z, keys, values, rates, weights)


def update_body(heads, count, z_ref, w_ref, m_ref, *refs):
    terms, w_out, m_out = refs[:count], refs[count], refs[count + 1]
    size = w_ref.shape[1] // (3 * heads)
    for g in range(3 * heads):
        cols = slice(g * size, (g + 1) * size)
        new = momentum_keep * m_ref[:, cols]
        for term in terms:
            new = new + term[:, cols].astype(jnp.float32)
        before = w_ref[:, cols].astype(jnp.float32)
        moved = before + new
        ratio = jnp.sqrt(
            (jnp.mean(before * before, axis=-1, keepdims=True) + epsilon)
            / (jnp.mean(moved * moved, axis=-1, keepdims=True) + epsilon)
        )
        m_out[:, cols] = new
        w_out[:, cols] = (moved * ratio).astype(w_out.dtype)


def updated(z, weights, momentum, terms, heads):
    own, width = momentum.shape
    whole = pl.BlockSpec((own, width), lambda i, z: (0, 0))
    return call(
        functools.partial(update_body, heads, len(terms)),
        "update",
        (1,),
        [pl.BlockSpec((own, width), lambda i, z: (z[0], 0)), whole] + [whole] * len(terms),
        [whole, whole],
        [
            jax.ShapeDtypeStruct((own, width), jnp.bfloat16),
            jax.ShapeDtypeStruct((own, width), jnp.float32),
        ],
        (),
        1,
        20 * own * width,
        16 * own * width,
    )(z, weights, momentum, *terms)


def tile_attention(query, segments):
    factor = query.shape[1] ** (-0.5)
    scores = []
    for key, _, mask in segments:
        score = dot(query, key, NT)
        scores.append(score if mask is None else jnp.where(mask, score, MASKED))
    top = functools.reduce(jnp.maximum, [jnp.max(s, axis=-1, keepdims=True) for s in scores])
    total, out = 0.0, 0.0
    for score, (_, value, _) in zip(scores, segments):
        weight = jnp.exp((score - top) * factor)
        total = total + jnp.sum(weight, axis=-1, keepdims=True)
        out = out + dot(weight.astype(jnp.bfloat16), value)
    return out / total, top * factor + jnp.log(total)


def masks():
    row = lax.broadcasted_iota(jnp.int32, (TILE, TILE), 0)
    col = lax.broadcasted_iota(jnp.int32, (TILE, TILE), 1)
    return col <= row, col > row


def local_segments(k_ref, v_ref, t, first):
    causal, late = masks()
    depth = WIN // TILE
    found = []
    for j in range(max(first, t - depth), t + 1):
        mask = causal if j == t else late if j == t - depth else None
        rows = slice(j * TILE, (j + 1) * TILE)
        found.append((k_ref[rows, :], v_ref[rows, :], mask))
    return found


def later_body(q_ref, k_ref, v_ref, o_ref):
    for t in range(WIN // TILE, q_ref.shape[0] // TILE):
        rows = slice(t * TILE, (t + 1) * TILE)
        out, _ = tile_attention(q_ref[rows, :], local_segments(k_ref, v_ref, t, 0))
        o_ref[t * TILE - WIN : (t + 1) * TILE - WIN, :] = out.astype(o_ref.dtype)


def later_blocks(queries, keys, values, heads, size):
    rows = queries.shape[0]
    column = pl.BlockSpec((rows, size), lambda h: (0, h))
    return call(
        later_body,
        "later",
        (heads,),
        [column] * 3,
        pl.BlockSpec((rows - WIN, size), lambda h: (0, h)),
        jax.ShapeDtypeStruct((rows - WIN, heads * size), jnp.bfloat16),
        flops=6 * (rows - WIN) * WIN * size * heads,
        nbytes=8 * rows * size * heads,
    )(queries, keys, values)


def carried_body(z_ref, q_ref, k_ref, v_ref, pk_ref, pv_ref, o_ref):
    causal, late = masks()
    depth = WIN // TILE
    there = z_ref[0] > 0
    for t in range(depth):
        rows = slice(t * TILE, (t + 1) * TILE)
        found = local_segments(k_ref, v_ref, t, 0)
        for j in range(t, depth):
            mask = (late & there) if j == t else there
            span = slice(j * TILE, (j + 1) * TILE)
            found.append((pk_ref[span, :], pv_ref[span, :], jnp.broadcast_to(mask, causal.shape)))
        out, _ = tile_attention(q_ref[rows, :], found)
        o_ref[rows, :] = out.astype(o_ref.dtype)


def carried_block(z, queries, keys, values, carried, size):
    heads = carried.shape[2] // size
    column = pl.BlockSpec((WIN, size), lambda h, z: (0, h))
    return call(
        carried_body,
        "carried",
        (heads,),
        [column] * 3
        + [pl.BlockSpec((None, WIN, size), lambda h, z, c=c: (c, 0, h)) for c in range(2)],
        column,
        jax.ShapeDtypeStruct((WIN, heads * size), jnp.bfloat16),
        (),
        1,
        6 * WIN * WIN * size * heads,
        10 * WIN * size * heads,
    )(z, queries, keys, values, carried, carried)


EXTRA = 16


def put_partial(o_ref, t, out, level):
    rows = slice(t * TILE, (t + 1) * TILE)
    o_ref[rows, :] = out.astype(o_ref.dtype)
    size = out.shape[1]
    lines = []
    for c in range(TILE // size):
        wide = jnp.broadcast_to(level[c * size : (c + 1) * size], (size, size))
        lines.append(jnp.transpose(wide)[:1])
    return lines


def put_levels(o_ref, lines):
    line = jnp.concatenate(lines, axis=0)
    rest = line
    parts = []
    for _ in range(3):
        part = rest.astype(jnp.bfloat16).astype(jnp.float32)
        parts.append(part)
        rest = rest - part
    parts.append(jnp.zeros((EXTRA - 3 * line.shape[0], line.shape[1]), jnp.float32))
    o_ref[WIN:, :] = jnp.concatenate(parts, axis=0).astype(o_ref.dtype)


def get_levels(o_ref):
    size = o_ref.shape[1]
    count = WIN // size
    block = o_ref[WIN:, :].astype(jnp.float32)
    return block[:count] + (block[count : 2 * count] + block[2 * count : 3 * count])


def own_part_body(q_ref, k_ref, v_ref, o_ref):
    lines = []
    for t in range(WIN // TILE):
        rows = slice(t * TILE, (t + 1) * TILE)
        out, level = tile_attention(q_ref[rows, :], local_segments(k_ref, v_ref, t, 0))
        lines += put_partial(o_ref, t, out, level)
    put_levels(o_ref, lines)


def next_part_body(q_ref, k_ref, v_ref, o_ref):
    _, late = masks()
    depth = WIN // TILE
    lines = []
    for t in range(depth):
        rows = slice(t * TILE, (t + 1) * TILE)
        found = []
        for j in range(t, depth):
            span = slice(j * TILE, (j + 1) * TILE)
            found.append((k_ref[span, :], v_ref[span, :], late if j == t else None))
        out, level = tile_attention(q_ref[rows, :], found)
        lines += put_partial(o_ref, t, out, level)
    put_levels(o_ref, lines)


def part(body, name, queries, skip, keys, values, heads, first, size, block):
    column = pl.BlockSpec((WIN, size), lambda h: (block, h + first))
    return call(
        body,
        name,
        (heads,),
        [pl.BlockSpec((WIN, size), lambda h: (0, h + skip)), column, column],
        pl.BlockSpec((WIN + EXTRA, size), lambda h: (0, h)),
        jax.ShapeDtypeStruct((WIN + EXTRA, heads * size), jnp.bfloat16),
        flops=4 * WIN * WIN * size * heads,
        nbytes=8 * WIN * size * heads,
    )(queries, keys, values)


def final_body(peers, kept, z_ref, q_ref, later_ref, carried_ref, own_ref, next_ref, *refs):
    blocks, o_ref, whole = refs[:peers], refs[peers], refs[peers + 1]
    head = pl.program_id(0)
    size = q_ref.shape[1]
    rows = blocks[0].shape[0]
    for m in range(peers):
        row = pl.multiple_of((z_ref[0] ^ m) * rows, rows)
        whole[pl.ds(row, rows), :] = blocks[m][...].astype(whole.dtype)
    weights = whole[...].astype(jnp.bfloat16)

    def network(query):
        inner = dot(query, weights[:, : 2 * size])
        gate, up = inner[:, :size], inner[:, size:]
        hidden = (gate * sigmoid(gate) * up).astype(jnp.bfloat16)
        return dot(hidden, weights[:, 2 * size :], NT)

    o_ref[WIN:, :] = (network(q_ref[WIN:, :]) + later_ref[...].astype(jnp.float32)).astype(
        o_ref.dtype
    )
    fast = network(q_ref[:WIN, :])

    @pl.when(head < kept)
    def _():
        o_ref[:WIN, :] = (fast + carried_ref[...].astype(jnp.float32)).astype(o_ref.dtype)

    @pl.when(head >= kept)
    def _():
        share = jax.nn.sigmoid(get_levels(next_ref) - get_levels(own_ref))
        share = jnp.where(z_ref[0] > 0, share, 0.0)
        for c in range(WIN // size):
            rows = slice(c * size, (c + 1) * size)
            weight = jnp.transpose(jnp.broadcast_to(share[c : c + 1], (size, size)))
            own = own_ref[rows, :].astype(jnp.float32)
            other = next_ref[rows, :].astype(jnp.float32)
            o_ref[rows, :] = (fast[rows] + own + weight * (other - own)).astype(o_ref.dtype)


def final(z, queries, later, carried, own_part, next_part, blocks, kept, size):
    rows, width = queries.shape
    heads = width // size
    peers, own = len(blocks), blocks[0].shape[0]
    column = pl.BlockSpec((rows, size), lambda h, z: (0, h))
    partial = pl.BlockSpec((WIN + EXTRA, size), lambda h, z: (0, jnp.maximum(h - kept, 0)))
    return call(
        functools.partial(final_body, peers, kept),
        "final",
        (heads,),
        [
            column,
            pl.BlockSpec((rows - WIN, size), lambda h, z: (0, h)),
            pl.BlockSpec((WIN, size), lambda h, z: (0, jnp.minimum(h, kept - 1))),
            partial,
            partial,
        ]
        + [pl.BlockSpec((own, 3 * size), lambda h, z: (0, h))] * peers,
        column,
        jax.ShapeDtypeStruct((rows, width), jnp.bfloat16),
        [pltpu.VMEM((size, 3 * size), jnp.bfloat16 if own % 16 == 0 else jnp.float32)],
        1,
        6 * rows * width * size,
        6 * rows * width,
    )(z, queries, later, carried, own_part, next_part, *blocks)


def moved_by(value, by):
    peers = lax.axis_size("seq")
    pairs = [(i, i + by) for i in range(peers) if 0 <= i + by < peers]
    return lax.ppermute(value, "seq", pairs)


def swapped(value, mask):
    return lax.ppermute(value, "seq", [(i, i ^ mask) for i in range(lax.axis_size("seq"))])


def shards(queries, keys, values, rates, fast_weights, momentum):
    rows = queries.shape[0]
    heads = rates.shape[0]
    size = fast_weights.shape[0]
    own = momentum.shape[0]
    peers = lax.axis_size("seq")
    kept = heads * 2 // 5
    z = lax.axis_index("seq").astype(jnp.int32).reshape(1)
    cut = kept * size

    carried = moved_by(jnp.stack([keys[rows - WIN :, :cut], values[rows - WIN :, :cut]]), 1)
    asked = moved_by(queries[:WIN, cut:], -1)

    flat = fast_weights.reshape(size, heads * 3 * size)
    flat_momentum = momentum.reshape(own, heads * 3 * size)
    kinds = [jnp.bfloat16 if m % 2 else jnp.float32 for m in range(peers)]
    sums = [[block] for block in partial_grads(z, keys, values, rates, flat, peers, kinds)]

    step = 1
    while step < peers:
        for m in reversed(range(peers)):
            if m % (2 * step) == step:
                terms = sums[m]
                block = functools.reduce(jnp.add, [t.astype(jnp.float32) for t in terms])
                sums[m - step].append(swapped(block.astype(jnp.bfloat16), step))
        step *= 2

    later = later_blocks(queries, keys, values, heads, size)
    own_part = part(own_part_body, "own_part", queries, kept, keys, values, heads - kept, kept, size, 0)
    given = part(
        next_part_body, "next_part", asked, 0, keys, values, heads - kept, kept, size, rows // WIN - 1
    )
    next_part = moved_by(given, 1)
    carried_out = carried_block(z, queries, keys, values, carried, size)

    new_flat, momentum_flat = updated(z, flat, flat_momentum, sums[0], heads)
    blocks = {0: new_flat}
    step = peers // 2
    while step:
        for m in sorted(blocks):
            blocks[m + step] = swapped(blocks[m], step)
        step //= 2
    blocks = [blocks[m] for m in range(peers)]

    mixed = final(z, queries, later, carried_out, own_part, next_part, blocks, kept, size)
    shape = momentum.shape
    return (mixed, new_flat.reshape(shape), momentum_flat.reshape(shape))


def solution(mesh):
    return jax.shard_map(
        shards,
        mesh=mesh,
        in_specs=(
            P(("groups", "seq"), ("head", "rep")),
            P(("groups", "seq"), ("head", "rep")),
            P(("groups", "seq"), ("head", "rep")),
            P(("head", "rep"), ("groups", "seq")),
            P(None, ("head", "rep"), None, None),
            P("seq", ("head", "rep"), None, None),
        ),
        out_specs=(
            P(("groups", "seq"), ("head", "rep")),
            P(("groups", "seq"), ("head", "rep"), None, None),
            P(("groups", "seq"), ("head", "rep"), None, None),
        ),
        check_vma=False,
    )
```

```python
import functools
import math

import jax
import jax.numpy as jnp
from jax import lax
from jax.experimental import pallas as pl
from jax.experimental.pallas import tpu as pltpu
from jax.sharding import PartitionSpec as P

WIN = 512
TILE = 256

momentum_keep = 0.9
epsilon = 1e-06
MASKED = -1e30
LOG2E = math.log2(math.e)
NT = (((1,), (1,)), ((), ()))


def call(body, name, grid, in_specs, out_specs, out_shape, scratch=(), prefetch=0, flops=0, nbytes=0):
    return pl.pallas_call(
        body,
        name=name,
        out_shape=out_shape,
        grid_spec=pltpu.PrefetchScalarGridSpec(
            num_scalar_prefetch=prefetch,
            grid=grid,
            in_specs=in_specs,
            out_specs=out_specs,
            scratch_shapes=list(scratch),
        ),
        cost_estimate=pl.CostEstimate(flops=flops, bytes_accessed=nbytes, transcendentals=0),
    )


def sigmoid(x):
    return 0.5 * jnp.tanh(0.5 * x) + 0.5


def dot(a, b, dims=None):
    if dims is None:
        return jnp.dot(a, b, preferred_element_type=jnp.float32)
    return lax.dot_general(a, b, dims, preferred_element_type=jnp.float32)


def steps_of(heads, most=5):
    return next(n for n in range(min(heads, most), 0, -1) if heads % n == 0)


def grad_body(peers, group, chunk, z_ref, k_ref, v_ref, r_ref, w_ref, *refs):
    outs, total = refs[:peers], refs[peers]
    size = w_ref.shape[2]
    rows = k_ref.shape[0]
    own = outs[0].shape[2]
    first = pl.program_id(0) * group
    tasks = [(g, c) for g in range(group) for c in range(0, rows, chunk)]
    turned = {}

    def products(g, c):
        if g not in turned:
            flipped = [jnp.transpose(w_ref[g, m]) for m in range(3)]
            turned[g] = (jnp.concatenate(flipped[:2], axis=0), flipped[2])
        cols, span = slice(g * size, (g + 1) * size), slice(c, c + chunk)
        inner = dot(turned[g][0], k_ref[span, cols], NT)
        return inner, dot(turned[g][1], v_ref[span, cols], NT)

    def finish(g, c, inner, back, sums):
        cols, span = slice(g * size, (g + 1) * size), slice(c, c + chunk)
        rate = r_ref[pl.ds(first + g, 1), span]
        gate, up = inner[:size], inner[size:]
        back = back * rate
        sig = sigmoid(gate)
        silu = gate * sig
        hidden = (silu * (up * rate)).astype(jnp.bfloat16)
        gate_grad = (back * up * (sig + silu * (1.0 - sig))).astype(jnp.bfloat16)
        up_grad = (back * silu).astype(jnp.bfloat16)
        found = [
            dot(jnp.concatenate([gate_grad, up_grad], axis=0), k_ref[span, cols]),
            dot(hidden, v_ref[span, cols]),
        ]
        sums = found if sums is None else [a + b for a, b in zip(sums, found)]
        if c + chunk < rows:
            return sums
        total[g % 2, 0] = jnp.transpose(sums[0][:size])
        total[g % 2, 1] = jnp.transpose(sums[0][size:])
        total[g % 2, 2] = jnp.transpose(sums[1])
        for m in range(peers):
            row = pl.multiple_of((z_ref[0] ^ m) * own, own)
            outs[m][g] = total[g % 2, :, pl.ds(row, own), :].astype(outs[m].dtype)
        return None

    sums = None
    ready = products(*tasks[0])
    for i, task in enumerate(tasks):
        following = products(*tasks[i + 1]) if i + 1 < len(tasks) else None
        sums = finish(*task, *ready, sums)
        ready = following


def partial_grads(z, keys, values, rates, weights, peers, kinds):
    rows = keys.shape[0]
    heads, _, size, _ = weights.shape
    own = size // peers
    group = steps_of(heads)
    column = pl.BlockSpec((rows, group * size), lambda h, z: (0, h))
    return call(
        functools.partial(grad_body, peers, group, min(rows, 512)),
        "grads",
        (heads // group,),
        [
            column,
            column,
            pl.BlockSpec((heads, rows), lambda h, z: (0, 0)),
            pl.BlockSpec((group, 3, size, size), lambda h, z: (h, 0, 0, 0)),
        ],
        [pl.BlockSpec((group, 3, own, size), lambda h, z: (h, 0, 0, 0))] * peers,
        [jax.ShapeDtypeStruct((heads, 3, own, size), kind) for kind in kinds],
        [pltpu.VMEM((2, 3, size, size), jnp.float32)],
        1,
        12 * rows * heads * size * size,
        4 * rows * heads * size,
    )(z, keys, values, rates, weights)


def update_body(count, z_ref, w_ref, m_ref, *refs):
    terms, w_out, m_out = refs[:count], refs[count], refs[count + 1]
    for g in range(w_ref.shape[0]):
        new = momentum_keep * m_ref[g]
        for term in terms:
            new = new + term[g].astype(jnp.float32)
        before = w_ref[g].astype(jnp.float32)
        moved = before + new
        ratio = jnp.sqrt(
            (jnp.mean(before * before, axis=-1, keepdims=True) + epsilon)
            / (jnp.mean(moved * moved, axis=-1, keepdims=True) + epsilon)
        )
        m_out[g] = new
        w_out[g] = (moved * ratio).astype(w_out.dtype)


def updated(z, weights, momentum, terms):
    shape = momentum.shape
    whole = pl.BlockSpec(shape, lambda i, z: (0, 0, 0, 0))
    count = momentum.size
    return call(
        functools.partial(update_body, len(terms)),
        "update",
        (1,),
        [pl.BlockSpec(shape, lambda i, z: (0, 0, z[0], 0)), whole] + [whole] * len(terms),
        [whole, whole],
        [jax.ShapeDtypeStruct(shape, jnp.bfloat16), jax.ShapeDtypeStruct(shape, jnp.float32)],
        (),
        1,
        20 * count,
        16 * count,
    )(z, weights, momentum, *terms)


def attend(tasks, s_ref):
    def scores(i):
        query, segments, _ = tasks[i]
        query = query()
        top = None
        for j, (key, _, mask) in enumerate(segments):
            score = dot(key(), query, NT)
            if mask is not None:
                score = jnp.where(mask, score, MASKED)
            s_ref[i % 2, j * TILE : (j + 1) * TILE, :] = score
            most = jnp.max(score.reshape(TILE // 8, 8, TILE), axis=0)
            top = most if top is None else jnp.maximum(top, most)
        return jnp.max(top, axis=0, keepdims=True)

    def weigh(i, top):
        _, segments, emit = tasks[i]
        factor = segments[0][0]().shape[1] ** (-0.5)
        out = total = None
        for j, (_, value, _) in enumerate(segments):
            score = s_ref[i % 2, j * TILE : (j + 1) * TILE, :]
            weight = jnp.exp2((score - top) * (factor * LOG2E))
            part = jnp.sum(weight.reshape(TILE // 8, 8, TILE), axis=0)
            product = dot(value(), weight.astype(jnp.bfloat16))
            total = part if total is None else total + part
            out = product if out is None else out + product
        total = jnp.sum(total, axis=0, keepdims=True)
        emit(out * (1.0 / total), top * factor + jnp.log(total))

    top = scores(0)
    for i in range(len(tasks)):
        following = scores(i + 1) if i + 1 < len(tasks) else None
        weigh(i, top)
        top = following


def masks():
    row = lax.broadcasted_iota(jnp.int32, (TILE, TILE), 0)
    col = lax.broadcasted_iota(jnp.int32, (TILE, TILE), 1)
    return row <= col, row > col


def spans(ref, t, cols):
    return lambda: ref[t * TILE : (t + 1) * TILE, cols]


def turned(memo, ref, t, cols, key):
    def load():
        if (key, t) not in memo:
            memo[key, t] = jnp.transpose(ref[t * TILE : (t + 1) * TILE, cols])
        return memo[key, t]

    return load


def put(o_ref, t, cols):
    def emit(out, level):
        o_ref[t * TILE : (t + 1) * TILE, cols] = jnp.transpose(out).astype(o_ref.dtype)

    return emit


SCORES = (WIN // TILE + 1) * TILE


def later_body(group, q_ref, k_ref, v_ref, o_ref, s_ref):
    size = q_ref.shape[1] // group
    causal, late = masks()
    depth = WIN // TILE
    tasks = []
    for g in range(group):
        cols = slice(g * size, (g + 1) * size)
        memo = {}
        for t in range(depth, q_ref.shape[0] // TILE):
            found = [
                (
                    spans(k_ref, j, cols),
                    turned(memo, v_ref, j, cols, 0),
                    causal if j == t else late if j == t - depth else None,
                )
                for j in range(t - depth, t + 1)
            ]
            tasks.append((spans(q_ref, t, cols), found, put(o_ref, t - depth, cols)))
    attend(tasks, s_ref)


def later_blocks(queries, keys, values, heads, size, first, group):
    rows = queries.shape[0]
    column = pl.BlockSpec((rows, group * size), lambda h: (0, first // group + h))
    return call(
        functools.partial(later_body, group),
        "later",
        (heads // group,),
        [column] * 3,
        pl.BlockSpec((rows - WIN, group * size), lambda h: (0, h)),
        jax.ShapeDtypeStruct((rows - WIN, heads * size), jnp.bfloat16),
        [pltpu.VMEM((2, SCORES, TILE), jnp.float32)],
        0,
        6 * (rows - WIN) * WIN * size * heads,
        8 * rows * size * heads,
    )(queries, keys, values)


def carried_body(group, z_ref, q_ref, k_ref, v_ref, pk_ref, pv_ref, o_ref, s_ref):
    size = q_ref.shape[1] // group
    causal, late = masks()
    depth = WIN // TILE
    there = jnp.broadcast_to(z_ref[0] > 0, causal.shape)
    tasks = []
    for g in range(group):
        cols = slice(g * size, (g + 1) * size)
        memo = {}
        for t in range(depth):
            found = [
                (spans(pk_ref, j, cols), turned(memo, pv_ref, j, cols, 1), late & there if j == t else there)
                for j in range(t, depth)
            ]
            found += [
                (spans(k_ref, j, cols), turned(memo, v_ref, j, cols, 0), causal if j == t else None)
                for j in range(t + 1)
            ]
            tasks.append((spans(q_ref, t, cols), found, put(o_ref, t, cols)))
    attend(tasks, s_ref)


def carried_block(z, queries, keys, values, carried, size):
    heads = carried.shape[2] // size
    group = steps_of(heads, 4)
    width = queries.shape[1]
    column = pl.BlockSpec((WIN, group * size), lambda h, z: (0, h))
    return call(
        functools.partial(carried_body, group),
        "carried",
        (heads // group,),
        [column] * 3
        + [pl.BlockSpec((None, WIN, group * size), lambda h, z, c=c: (c, 0, h)) for c in range(2)],
        column,
        jax.ShapeDtypeStruct((WIN, width), jnp.bfloat16),
        [pltpu.VMEM((2, SCORES, TILE), jnp.float32)],
        1,
        6 * WIN * WIN * size * heads,
        10 * WIN * size * heads,
    )(z, queries, keys, values, carried, carried)


EXTRA = 16


def put_partial(o_ref, g, t, size):
    def emit(out, level):
        span = slice(t * TILE, (t + 1) * TILE)
        o_ref[g, :size, span] = out.astype(o_ref.dtype)
        rest, parts = level, []
        for _ in range(3):
            term = rest.astype(jnp.bfloat16).astype(jnp.float32)
            parts.append(term)
            rest = rest - term
        parts.append(jnp.zeros((EXTRA - 3, TILE), jnp.float32))
        o_ref[g, size:, span] = jnp.concatenate(parts, axis=0).astype(o_ref.dtype)

    return emit


def next_part_body(group, q_ref, k_ref, v_ref, o_ref, s_ref):
    size = q_ref.shape[1] // group
    _, late = masks()
    depth = WIN // TILE
    tasks = []
    for g in range(group):
        cols = slice(g * size, (g + 1) * size)
        memo = {}
        for t in range(depth):
            found = [
                (spans(k_ref, j, cols), turned(memo, v_ref, j, cols, 0), late if j == t else None)
                for j in range(t, depth)
            ]
            tasks.append((spans(q_ref, t, cols), found, put_partial(o_ref, g, t, size)))
    attend(tasks, s_ref)


def next_part(asked, keys, values, first, size):
    heads = asked.shape[1] // size
    block = keys.shape[0] // WIN - 1
    group = math.gcd(heads, first)
    column = pl.BlockSpec((WIN, group * size), lambda h: (block, h + first // group))
    return call(
        functools.partial(next_part_body, group),
        "next_part",
        (heads // group,),
        [pl.BlockSpec((WIN, group * size), lambda h: (0, h)), column, column],
        pl.BlockSpec((group, size + EXTRA, WIN), lambda h: (h, 0, 0)),
        jax.ShapeDtypeStruct((heads, size + EXTRA, WIN), jnp.bfloat16),
        [pltpu.VMEM((2, WIN, TILE), jnp.float32)],
        0,
        4 * WIN * WIN * size * heads,
        8 * WIN * size * heads,
    )(asked, keys, values)


def joined_body(group, z_ref, q_ref, k_ref, v_ref, p_ref, _, o_ref, s_ref):
    size = q_ref.shape[1] // group
    causal, _ = masks()
    depth = WIN // TILE

    def join(g, t, cols):
        def emit(out, level):
            span = slice(t * TILE, (t + 1) * TILE)
            terms = p_ref[g, size:, span].astype(jnp.float32)
            other = terms[0:1] + (terms[1:2] + terms[2:3])
            share = jnp.where(z_ref[0] > 0, jax.nn.sigmoid(other - level), 0.0)
            out = out + share * (p_ref[g, :size, span].astype(jnp.float32) - out)
            o_ref[span, cols] = jnp.transpose(out).astype(o_ref.dtype)

        return emit

    tasks = []
    for g in range(group):
        cols = slice(g * size, (g + 1) * size)
        memo = {}
        for t in range(depth):
            found = [
                (spans(k_ref, j, cols), turned(memo, v_ref, j, cols, 0), causal if j == t else None)
                for j in range(t + 1)
            ]
            tasks.append((spans(q_ref, t, cols), found, join(g, t, cols)))
    attend(tasks, s_ref)


def joined_block(z, queries, keys, values, given, partly, first, size):
    heads = given.shape[0]
    group = math.gcd(heads, first)
    column = pl.BlockSpec((WIN, group * size), lambda h, z: (0, h + first // group))
    return pl.pallas_call(
        functools.partial(joined_body, group),
        name="joined",
        out_shape=jax.ShapeDtypeStruct(partly.shape, partly.dtype),
        grid_spec=pltpu.PrefetchScalarGridSpec(
            num_scalar_prefetch=1,
            grid=(heads // group,),
            in_specs=[
                column,
                column,
                column,
                pl.BlockSpec((group, size + EXTRA, WIN), lambda h, z: (h, 0, 0)),
                pl.BlockSpec(memory_space=pl.ANY),
            ],
            out_specs=column,
            scratch_shapes=[pltpu.VMEM((2, WIN, TILE), jnp.float32)],
        ),
        input_output_aliases={5: 0},
        cost_estimate=pl.CostEstimate(
            flops=4 * WIN * WIN * size * heads, bytes_accessed=10 * WIN * size * heads, transcendentals=0
        ),
    )(z, queries, keys, values, given, partly)


def final_body(peers, group, z_ref, q_ref, first_ref, later_ref, *refs):
    blocks, o_ref, whole = refs[:peers], refs[peers], refs[peers + 1]
    size = q_ref.shape[1] // group
    own = blocks[0].shape[2]
    for m in range(peers):
        row = pl.multiple_of((z_ref[0] ^ m) * own, own)
        whole[:, :, pl.ds(row, own), :] = blocks[m][...].astype(whole.dtype)
    tasks = [(g, c) for g in range(group) for c in range(0, q_ref.shape[0], WIN)]

    def products(g, c):
        query = q_ref[c : c + WIN, g * size : (g + 1) * size]
        both = jnp.concatenate([whole[g, 0], whole[g, 1]], axis=1).astype(jnp.bfloat16)
        return dot(query, both)

    def finish(g, c, inner):
        cols = slice(g * size, (g + 1) * size)
        gate, up = inner[:, :size], inner[:, size:]
        hidden = (gate * sigmoid(gate) * up).astype(jnp.bfloat16)
        fast = dot(hidden, whole[g, 2].astype(jnp.bfloat16), NT)
        kept = first_ref[:, cols] if c == 0 else later_ref[c - WIN : c, cols]
        o_ref[c : c + WIN, cols] = (fast + kept.astype(jnp.float32)).astype(o_ref.dtype)

    ready = products(*tasks[0])
    for i, task in enumerate(tasks):
        following = products(*tasks[i + 1]) if i + 1 < len(tasks) else None
        finish(*task, ready)
        ready = following


def final(z, queries, first, later, blocks, size):
    rows, width = queries.shape
    heads = width // size
    group = steps_of(heads)
    peers, own = len(blocks), blocks[0].shape[2]
    column = pl.BlockSpec((rows, group * size), lambda h, z: (0, h))
    kind = jnp.bfloat16 if own % 16 == 0 else jnp.float32
    return call(
        functools.partial(final_body, peers, group),
        "final",
        (heads // group,),
        [
            column,
            pl.BlockSpec((WIN, group * size), lambda h, z: (0, h)),
            pl.BlockSpec((rows - WIN, group * size), lambda h, z: (0, h)),
        ]
        + [pl.BlockSpec((group, 3, own, size), lambda h, z: (h, 0, 0, 0))] * peers,
        column,
        jax.ShapeDtypeStruct((rows, width), jnp.bfloat16),
        [pltpu.VMEM((group, 3, size, size), kind)],
        1,
        6 * rows * width * size,
        6 * rows * width,
    )(z, queries, first, later, *blocks)


def moved_by(value, by):
    peers = lax.axis_size("seq")
    pairs = [(i, i + by) for i in range(peers) if 0 <= i + by < peers]
    return lax.ppermute(value, "seq", pairs)


def swapped(value, mask):
    return lax.ppermute(value, "seq", [(i, i ^ mask) for i in range(lax.axis_size("seq"))])


def shards(queries, keys, values, rates, fast_weights, momentum):
    rows = queries.shape[0]
    heads = rates.shape[0]
    size = fast_weights.shape[0]
    peers = lax.axis_size("seq")
    kept = heads * 2 // 5
    z = lax.axis_index("seq").astype(jnp.int32).reshape(1)
    cut = kept * size

    carried = moved_by(jnp.stack([keys[rows - WIN :, :cut], values[rows - WIN :, :cut]]), 1)
    asked = moved_by(queries[:WIN, cut:], -1)

    weights = jnp.transpose(fast_weights, (1, 2, 0, 3))
    own_momentum = jnp.transpose(momentum, (1, 2, 0, 3))
    kinds = [jnp.bfloat16 if m % 2 else jnp.float32 for m in range(peers)]
    sums = [[block] for block in partial_grads(z, keys, values, rates, weights, peers, kinds)]

    step = 1
    while step < peers:
        for m in reversed(range(peers)):
            if m % (2 * step) == step:
                terms = sums[m]
                block = functools.reduce(jnp.add, [t.astype(jnp.float32) for t in terms])
                sums[m - step].append(swapped(block.astype(jnp.bfloat16), step))
        step *= 2

    later = later_blocks(queries, keys, values, heads, size, 0, steps_of(heads))
    given = moved_by(next_part(asked, keys, values, kept, size), 1)
    first = carried_block(z, queries, keys, values, carried, size)
    first = joined_block(z, queries, keys, values, given, first, kept, size)

    new_rows, new_momentum = updated(z, weights, own_momentum, sums[0])
    blocks = {0: new_rows}
    step = peers // 2
    while step:
        for m in sorted(blocks):
            blocks[m + step] = swapped(blocks[m], step)
        step //= 2
    blocks = [blocks[m] for m in range(peers)]

    mixed = final(z, queries, first, later, blocks, size)
    return (mixed, jnp.transpose(new_rows, (2, 0, 1, 3)), jnp.transpose(new_momentum, (2, 0, 1, 3)))


def solution(mesh):
    return jax.shard_map(
        shards,
        mesh=mesh,
        in_specs=(
            P(("groups", "seq"), ("head", "rep")),
            P(("groups", "seq"), ("head", "rep")),
            P(("groups", "seq"), ("head", "rep")),
            P(("head", "rep"), ("groups", "seq")),
            P(None, ("head", "rep"), None, None),
            P("seq", ("head", "rep"), None, None),
        ),
        out_specs=(
            P(("groups", "seq"), ("head", "rep")),
            P(("groups", "seq"), ("head", "rep"), None, None),
            P(("groups", "seq"), ("head", "rep"), None, None),
        ),
        check_vma=False,
    )
```

```python
import functools
import math

import jax
import jax.numpy as jnp
from jax import lax
from jax.experimental import pallas as pl
from jax.experimental.pallas import tpu as pltpu
from jax.sharding import PartitionSpec as P


WIN = 512
TILE = 256

momentum_keep = 0.9
epsilon = 1e-06
MASKED = -1e30
LOG2E = math.log2(math.e)
VMEM = pl.BlockSpec(memory_space=pltpu.VMEM)
NT = (((1,), (1,)), ((), ()))


def call(body, grid, in_specs, out_specs, out_shape, scratch=(), prefetch=0, flops=0, nbytes=0):
    return pl.pallas_call(
        body,
        out_shape=out_shape,
        grid_spec=pltpu.PrefetchScalarGridSpec(
            num_scalar_prefetch=prefetch,
            grid=grid,
            in_specs=in_specs,
            out_specs=out_specs,
            scratch_shapes=list(scratch),
        ),
        cost_estimate=pl.CostEstimate(flops=flops, bytes_accessed=nbytes, transcendentals=0),
    )


def sigmoid(x):
    return 0.5 * jnp.tanh(0.5 * x) + 0.5


def dot(a, b, dims=None):
    if dims is None:
        return jnp.dot(a, b, preferred_element_type=jnp.float32)
    return lax.dot_general(a, b, dims, preferred_element_type=jnp.float32)


def steps_of(heads, most=5):
    return next(n for n in range(min(heads, most), 0, -1) if heads % n == 0)


def grad_body(peers, group, chunk, z_ref, k_ref, v_ref, r_ref, w_ref, *refs):
    outs, total = refs[:peers], refs[peers]
    size = w_ref.shape[2]
    rows = k_ref.shape[0]
    own = outs[0].shape[2]
    first = pl.program_id(0) * group
    tasks = [(g, c) for g in range(group) for c in range(0, rows, chunk)]
    turned = {}

    def products(g, c):
        if g not in turned:
            flipped = [jnp.transpose(w_ref[g, m]) for m in range(3)]
            turned[g] = (jnp.concatenate(flipped[:2], axis=0), flipped[2])
        cols, span = slice(g * size, (g + 1) * size), slice(c, c + chunk)
        inner = dot(turned[g][0], k_ref[span, cols], NT)
        return inner, dot(turned[g][1], v_ref[span, cols], NT)

    def finish(g, c, inner, back, sums):
        cols, span = slice(g * size, (g + 1) * size), slice(c, c + chunk)
        rate = r_ref[pl.ds(first + g, 1), span]
        gate, up = inner[:size], inner[size:]
        back = back * rate
        sig = sigmoid(gate)
        silu = gate * sig
        hidden = (silu * (up * rate)).astype(jnp.bfloat16)
        gate_grad = (back * up * (sig + silu * (1.0 - sig))).astype(jnp.bfloat16)
        up_grad = (back * silu).astype(jnp.bfloat16)
        found = [
            dot(jnp.concatenate([gate_grad, up_grad], axis=0), k_ref[span, cols]),
            dot(hidden, v_ref[span, cols]),
        ]
        sums = found if sums is None else [a + b for a, b in zip(sums, found)]
        if c + chunk < rows:
            return sums
        total[g % 2, 0] = jnp.transpose(sums[0][:size])
        total[g % 2, 1] = jnp.transpose(sums[0][size:])
        total[g % 2, 2] = jnp.transpose(sums[1])
        for m in range(peers):
            row = pl.multiple_of((z_ref[0] ^ m) * own, own)
            outs[m][g] = total[g % 2, :, pl.ds(row, own), :].astype(outs[m].dtype)
        return None

    sums = None
    ready = products(*tasks[0])
    for i, task in enumerate(tasks):
        following = products(*tasks[i + 1]) if i + 1 < len(tasks) else None
        sums = finish(*task, *ready, sums)
        ready = following


def partial_grads(z, keys, values, rates, weights, peers, kinds):
    rows = keys.shape[0]
    heads, _, size, _ = weights.shape
    own = size // peers
    group = steps_of(heads)
    column = pl.BlockSpec((rows, group * size), lambda h, z: (0, h))
    return call(
        functools.partial(grad_body, peers, group, min(rows, 512)),
        (heads // group,),
        [
            column,
            column,
            pl.BlockSpec((heads, rows), lambda h, z: (0, 0)),
            pl.BlockSpec((group, 3, size, size), lambda h, z: (h, 0, 0, 0)),
        ],
        [pl.BlockSpec((group, 3, own, size), lambda h, z: (h, 0, 0, 0))] * peers,
        [jax.ShapeDtypeStruct((heads, 3, own, size), kind) for kind in kinds],
        [pltpu.VMEM((2, 3, size, size), jnp.float32)],
        1,
        12 * rows * heads * size * size,
        4 * rows * heads * size,
    )(z, keys, values, rates, weights)


def update_body(count, z_ref, w_ref, m_ref, *refs):
    terms, w_out, m_out = refs[:count], refs[count], refs[count + 1]
    for g in range(w_ref.shape[0]):
        new = momentum_keep * m_ref[g]
        for term in terms:
            new = new + term[g].astype(jnp.float32)
        before = w_ref[g].astype(jnp.float32)
        moved = before + new
        ratio = jnp.sqrt(
            (jnp.mean(before * before, axis=-1, keepdims=True) + epsilon)
            / (jnp.mean(moved * moved, axis=-1, keepdims=True) + epsilon)
        )
        m_out[g] = new
        w_out[g] = (moved * ratio).astype(w_out.dtype)


def updated(z, weights, momentum, terms):
    shape = momentum.shape
    whole = pl.BlockSpec(shape, lambda i, z: (0, 0, 0, 0))
    count = momentum.size
    return call(
        functools.partial(update_body, len(terms)),
        (1,),
        [pl.BlockSpec(shape, lambda i, z: (0, 0, z[0], 0)), whole] + [VMEM] * len(terms),
        [VMEM, whole],
        [jax.ShapeDtypeStruct(shape, jnp.bfloat16), jax.ShapeDtypeStruct(shape, jnp.float32)],
        (),
        1,
        20 * count,
        16 * count,
    )(z, weights, momentum, *terms)


def attend(tasks, s_ref):
    def scores(i):
        query, segments, _ = tasks[i]
        query = query()
        top = None
        for j, (key, _, mask) in enumerate(segments):
            score = dot(key(), query, NT)
            if mask is not None:
                score = jnp.where(mask, score, MASKED)
            s_ref[i % 2, j * TILE : (j + 1) * TILE, :] = score
            most = jnp.max(score.reshape(TILE // 8, 8, TILE), axis=0)
            top = most if top is None else jnp.maximum(top, most)
        return jnp.max(top, axis=0, keepdims=True)

    def weigh(i, top):
        _, segments, emit = tasks[i]
        factor = segments[0][0]().shape[1] ** (-0.5)
        out = total = None
        for j, (_, value, _) in enumerate(segments):
            score = s_ref[i % 2, j * TILE : (j + 1) * TILE, :]
            weight = jnp.exp2((score - top) * (factor * LOG2E))
            part = jnp.sum(weight.reshape(TILE // 8, 8, TILE), axis=0)
            product = dot(value(), weight.astype(jnp.bfloat16))
            total = part if total is None else total + part
            out = product if out is None else out + product
        total = jnp.sum(total, axis=0, keepdims=True)
        emit(out * (1.0 / total), top * factor + jnp.log(total))

    top = scores(0)
    for i in range(len(tasks)):
        following = scores(i + 1) if i + 1 < len(tasks) else None
        weigh(i, top)
        top = following


def masks():
    row = lax.broadcasted_iota(jnp.int32, (TILE, TILE), 0)
    col = lax.broadcasted_iota(jnp.int32, (TILE, TILE), 1)
    return row <= col, row > col


def spans(ref, t, cols):
    return lambda: ref[t * TILE : (t + 1) * TILE, cols]


def turned(memo, ref, t, cols, key):
    def load():
        if (key, t) not in memo:
            memo[key, t] = jnp.transpose(ref[t * TILE : (t + 1) * TILE, cols])
        return memo[key, t]

    return load


def put(o_ref, t, cols):
    def emit(out, level):
        o_ref[t * TILE : (t + 1) * TILE, cols] = jnp.transpose(out).astype(o_ref.dtype)

    return emit


SCORES = (WIN // TILE + 1) * TILE


def later_body(group, q_ref, k_ref, v_ref, *refs):
    o_ref, s_ref = refs[-2:]
    size = q_ref.shape[1] // group
    causal, late = masks()
    depth = WIN // TILE
    tasks = []
    for g in range(group):
        cols = slice(g * size, (g + 1) * size)
        memo = {}
        for t in range(depth, q_ref.shape[0] // TILE):
            found = [
                (
                    spans(k_ref, j, cols),
                    turned(memo, v_ref, j, cols, 0),
                    causal if j == t else late if j == t - depth else None,
                )
                for j in range(t - depth, t + 1)
            ]
            tasks.append((spans(q_ref, t, cols), found, put(o_ref, t - depth, cols)))
    attend(tasks, s_ref)


def later_blocks(queries, keys, values, size, step, group, partly):
    rows, width = queries.shape
    column = pl.BlockSpec((rows, group * size), lambda h: (0, step))
    more = [] if partly is None else [partly]
    return pl.pallas_call(
        functools.partial(later_body, group),
        name="later",
        out_shape=jax.ShapeDtypeStruct((rows - WIN, width), jnp.bfloat16),
        grid_spec=pltpu.PrefetchScalarGridSpec(
            num_scalar_prefetch=0,
            grid=(1,),
            in_specs=[column] * 3 + [pl.BlockSpec(memory_space=pl.ANY)] * len(more),
            out_specs=pl.BlockSpec((rows - WIN, group * size), lambda h: (0, step)),
            scratch_shapes=[pltpu.VMEM((2, SCORES, TILE), jnp.float32)],
        ),
        input_output_aliases={3: 0} if more else {},
        cost_estimate=pl.CostEstimate(
            flops=6 * (rows - WIN) * WIN * size * group,
            bytes_accessed=8 * rows * size * group,
            transcendentals=0,
        ),
    )(queries, keys, values, *more)


def carried_body(group, z_ref, q_ref, k_ref, v_ref, p_ref, o_ref, s_ref):
    size = q_ref.shape[1] // group
    causal, late = masks()
    depth = WIN // TILE
    there = jnp.broadcast_to(z_ref[0] > 0, causal.shape)
    tasks = []
    for g in range(group):
        cols = slice(g * size, (g + 1) * size)
        memo = {}
        for t in range(depth):
            found = [
                (spans(p_ref.at[0], j, cols), turned(memo, p_ref.at[1], j, cols, 1), late & there if j == t else there)
                for j in range(t, depth)
            ]
            found += [
                (spans(k_ref, j, cols), turned(memo, v_ref, j, cols, 0), causal if j == t else None)
                for j in range(t + 1)
            ]
            tasks.append((spans(q_ref, t, cols), found, put(o_ref, t, cols)))
    attend(tasks, s_ref)


def carried_block(z, queries, keys, values, carried, size):
    heads = carried.shape[2] // size
    group = heads
    width = queries.shape[1]
    column = pl.BlockSpec((WIN, group * size), lambda h, z: (0, h))
    return call(
        functools.partial(carried_body, group),
        (heads // group,),
        [column] * 3 + [VMEM],
        column,
        jax.ShapeDtypeStruct((WIN, width), jnp.bfloat16),
        [pltpu.VMEM((2, SCORES, TILE), jnp.float32)],
        1,
        6 * WIN * WIN * size * heads,
        10 * WIN * size * heads,
    )(z, queries, keys, values, carried)


EXTRA = 16


def put_partial(o_ref, g, t, size):
    def emit(out, level):
        span = slice(t * TILE, (t + 1) * TILE)
        o_ref[g, :size, span] = out.astype(o_ref.dtype)
        rest, parts = level, []
        for _ in range(3):
            term = rest.astype(jnp.bfloat16).astype(jnp.float32)
            parts.append(term)
            rest = rest - term
        parts.append(jnp.zeros((EXTRA - 3, TILE), jnp.float32))
        o_ref[g, size:, span] = jnp.concatenate(parts, axis=0).astype(o_ref.dtype)

    return emit


def next_part_body(group, q_ref, k_ref, v_ref, o_ref, s_ref):
    size = q_ref.shape[1] // group
    _, late = masks()
    depth = WIN // TILE
    tasks = []
    for g in range(group):
        cols = slice(g * size, (g + 1) * size)
        memo = {}
        for t in range(depth):
            found = [
                (spans(k_ref, j, cols), turned(memo, v_ref, j, cols, 0), late if j == t else None)
                for j in range(t, depth)
            ]
            tasks.append((spans(q_ref, t, cols), found, put_partial(o_ref, g, t, size)))
    attend(tasks, s_ref)


def next_part(asked, keys, values, first, size):
    heads = asked.shape[1] // size
    block = keys.shape[0] // WIN - 1
    group = math.gcd(heads, first)
    column = pl.BlockSpec((WIN, group * size), lambda h: (block, h + first // group))
    return call(
        functools.partial(next_part_body, group),
        (heads // group,),
        [pl.BlockSpec((WIN, group * size), lambda h: (0, h)), column, column],
        pl.BlockSpec((group, size + EXTRA, WIN), lambda h: (h, 0, 0)),
        jax.ShapeDtypeStruct((heads, size + EXTRA, WIN), jnp.bfloat16),
        [pltpu.VMEM((2, WIN, TILE), jnp.float32)],
        0,
        4 * WIN * WIN * size * heads,
        8 * WIN * size * heads,
    )(asked, keys, values)


def joined_body(group, z_ref, q_ref, k_ref, v_ref, p_ref, _, o_ref, s_ref):
    size = q_ref.shape[1] // group
    causal, _ = masks()
    depth = WIN // TILE
    step = pl.program_id(0) * group

    def join(g, t, cols):
        def emit(out, level):
            span = slice(t * TILE, (t + 1) * TILE)
            terms = p_ref[step + g, size:, span].astype(jnp.float32)
            other = terms[0:1] + (terms[1:2] + terms[2:3])
            share = jnp.where(z_ref[0] > 0, jax.nn.sigmoid(other - level), 0.0)
            out = out + share * (p_ref[step + g, :size, span].astype(jnp.float32) - out)
            o_ref[span, cols] = jnp.transpose(out).astype(o_ref.dtype)

        return emit

    tasks = []
    for g in range(group):
        cols = slice(g * size, (g + 1) * size)
        memo = {}
        for t in range(depth):
            found = [
                (spans(k_ref, j, cols), turned(memo, v_ref, j, cols, 0), causal if j == t else None)
                for j in range(t + 1)
            ]
            tasks.append((spans(q_ref, t, cols), found, join(g, t, cols)))
    attend(tasks, s_ref)


def joined_block(z, queries, keys, values, given, partly, first, size):
    heads = given.shape[0]
    group = math.gcd(heads, first)
    column = pl.BlockSpec((WIN, group * size), lambda h, z: (0, h + first // group))
    return pl.pallas_call(
        functools.partial(joined_body, group),
        name="joined",
        out_shape=jax.ShapeDtypeStruct(partly.shape, partly.dtype),
        grid_spec=pltpu.PrefetchScalarGridSpec(
            num_scalar_prefetch=1,
            grid=(heads // group,),
            in_specs=[
                column,
                column,
                column,
                VMEM,
                pl.BlockSpec(memory_space=pl.ANY),
            ],
            out_specs=column,
            scratch_shapes=[pltpu.VMEM((2, WIN, TILE), jnp.float32)],
        ),
        input_output_aliases={5: 0},
        cost_estimate=pl.CostEstimate(
            flops=4 * WIN * WIN * size * heads, bytes_accessed=10 * WIN * size * heads, transcendentals=0
        ),
    )(z, queries, keys, values, given, partly)


def final_body(peers, group, z_ref, q_ref, first_ref, later_ref, *refs):
    blocks, o_ref, whole = refs[:peers], refs[peers], refs[peers + 1]
    size = q_ref.shape[1] // group
    own = blocks[0].shape[2]
    start = pl.program_id(0) * group
    for m in range(peers):
        row = pl.multiple_of((z_ref[0] ^ m) * own, own)
        whole[:, :, pl.ds(row, own), :] = blocks[m][pl.ds(start, group)].astype(whole.dtype)
    tasks = [(g, c) for g in range(group) for c in range(0, q_ref.shape[0], WIN)]

    def products(g, c):
        query = q_ref[c : c + WIN, g * size : (g + 1) * size]
        both = jnp.concatenate([whole[g, 0], whole[g, 1]], axis=1).astype(jnp.bfloat16)
        return dot(query, both)

    def finish(g, c, inner):
        cols = slice(g * size, (g + 1) * size)
        gate, up = inner[:, :size], inner[:, size:]
        hidden = (gate * sigmoid(gate) * up).astype(jnp.bfloat16)
        fast = dot(hidden, whole[g, 2].astype(jnp.bfloat16), NT)
        kept = first_ref[:, cols] if c == 0 else later_ref[c - WIN : c, cols]
        o_ref[c : c + WIN, cols] = (fast + kept.astype(jnp.float32)).astype(o_ref.dtype)

    ready = products(*tasks[0])
    for i, task in enumerate(tasks):
        following = products(*tasks[i + 1]) if i + 1 < len(tasks) else None
        finish(*task, ready)
        ready = following


def final(z, queries, first, later, blocks, size):
    rows, width = queries.shape
    heads = width // size
    group = steps_of(heads)
    peers, own = len(blocks), blocks[0].shape[2]
    column = pl.BlockSpec((rows, group * size), lambda h, z: (0, h))
    kind = jnp.bfloat16 if own % 16 == 0 else jnp.float32
    return call(
        functools.partial(final_body, peers, group),
        (heads // group,),
        [
            column,
            pl.BlockSpec((WIN, group * size), lambda h, z: (0, h)),
            pl.BlockSpec((rows - WIN, group * size), lambda h, z: (0, h)),
        ]
        + [VMEM] * peers,
        column,
        jax.ShapeDtypeStruct((rows, width), jnp.bfloat16),
        [pltpu.VMEM((group, 3, size, size), kind)],
        1,
        6 * rows * width * size,
        6 * rows * width,
    )(z, queries, first, later, *blocks)


def moved_by(value, by):
    peers = lax.axis_size("seq")
    pairs = [(i, i + by) for i in range(peers) if 0 <= i + by < peers]
    return lax.ppermute(value, "seq", pairs)


def swapped(value, mask):
    return lax.ppermute(value, "seq", [(i, i ^ mask) for i in range(lax.axis_size("seq"))])


def kept_of(heads):
    return max(1, heads * 4 // 10)


def shards(queries, keys, values, rates, fast_weights, momentum):
    rows = queries.shape[0]
    heads = rates.shape[0]
    size = fast_weights.shape[0]
    peers = lax.axis_size("seq")
    kept = kept_of(heads)
    z = lax.axis_index("seq").astype(jnp.int32).reshape(1)
    cut = kept * size

    asked = moved_by(queries[:WIN, cut:], -1)
    carried = moved_by(jnp.stack([keys[rows - WIN :, :cut], values[rows - WIN :, :cut]]), 1)

    weights = jnp.transpose(fast_weights, (1, 2, 0, 3))
    own_momentum = jnp.transpose(momentum, (1, 2, 0, 3))
    kinds = [jnp.bfloat16 if m % 2 else jnp.float32 for m in range(peers)]
    sums = [[block] for block in partial_grads(z, keys, values, rates, weights, peers, kinds)]

    step = 1
    while step < peers:
        for m in reversed(range(peers)):
            if m % (2 * step) == step:
                terms = sums[m]
                block = functools.reduce(jnp.add, [t.astype(jnp.float32) for t in terms])
                sums[m - step].append(swapped(block.astype(jnp.bfloat16), step))
        step *= 2

    group = steps_of(heads)
    later = None
    for part in range(heads // group):
        later = later_blocks(queries, keys, values, size, part, group, later)
    given = next_part(asked, keys, values, kept, size)
    given = moved_by(given, 1)
    first = carried_block(z, queries, keys, values, carried, size)
    first = joined_block(z, queries, keys, values, given, first, kept, size)

    new_rows, new_momentum = updated(z, weights, own_momentum, sums[0])
    blocks = {0: new_rows}
    step = peers // 2
    while step:
        for m in sorted(blocks):
            blocks[m + step] = swapped(blocks[m], step)
        step //= 2
    blocks = [blocks[m] for m in range(peers)]

    mixed = final(z, queries, first, later, blocks, size)
    return (mixed, jnp.transpose(new_rows, (2, 0, 1, 3)), jnp.transpose(new_momentum, (2, 0, 1, 3)))


def solution(mesh):
    return jax.shard_map(
        shards,
        mesh=mesh,
        in_specs=(
            P(("groups", "seq"), ("head", "rep")),
            P(("groups", "seq"), ("head", "rep")),
            P(("groups", "seq"), ("head", "rep")),
            P(("head", "rep"), ("groups", "seq")),
            P(None, ("head", "rep"), None, None),
            P("seq", ("head", "rep"), None, None),
        ),
        out_specs=(
            P(("groups", "seq"), ("head", "rep")),
            P(("groups", "seq"), ("head", "rep"), None, None),
            P(("groups", "seq"), ("head", "rep"), None, None),
        ),
        check_vma=False,
    )
```

```python
import functools
import math

import jax
import jax.numpy as jnp
from jax import lax
from jax.experimental import pallas as pl
from jax.experimental.pallas import tpu as pltpu
from jax.sharding import PartitionSpec as P


WIN = 512
TILE = 256

momentum_keep = 0.9
epsilon = 1e-06
MASKED = -1e30
LOG2E = math.log2(math.e)
PARAMS = pltpu.CompilerParams(vmem_limit_bytes=24 * 2**20)
VMEM = pl.BlockSpec(memory_space=pltpu.VMEM)
NT = (((1,), (1,)), ((), ()))


def call(body, grid, in_specs, out_specs, out_shape, scratch=(), prefetch=0, flops=0, nbytes=0):
    return pl.pallas_call(
        body,
        out_shape=out_shape,
        grid_spec=pltpu.PrefetchScalarGridSpec(
            num_scalar_prefetch=prefetch,
            grid=grid,
            in_specs=in_specs,
            out_specs=out_specs,
            scratch_shapes=list(scratch),
        ),
        compiler_params=PARAMS,
        cost_estimate=pl.CostEstimate(flops=flops, bytes_accessed=nbytes, transcendentals=0),
    )


def far(x):
    return pltpu.with_memory_space_constraint(x, pltpu.HBM)


def sigmoid(x):
    return 0.5 * jnp.tanh(0.5 * x) + 0.5


def dot(a, b, dims=None):
    if dims is None:
        return jnp.dot(a, b, preferred_element_type=jnp.float32)
    return lax.dot_general(a, b, dims, preferred_element_type=jnp.float32)


def steps_of(heads, most=5):
    return next(n for n in range(min(heads, most), 0, -1) if heads % n == 0)


def grad_body(peers, group, chunk, z_ref, k_ref, v_ref, r_ref, w_ref, *refs):
    outs, total = refs[:peers], refs[peers]
    size = w_ref.shape[2]
    rows = k_ref.shape[0]
    own = outs[0].shape[2]
    first = pl.program_id(0) * group
    tasks = [(g, c) for g in range(group) for c in range(0, rows, chunk)]
    turned = {}

    def products(g, c):
        if g not in turned:
            flipped = [jnp.transpose(w_ref[g, m]) for m in range(3)]
            turned[g] = (jnp.concatenate(flipped[:2], axis=0), flipped[2])
        cols, span = slice(g * size, (g + 1) * size), slice(c, c + chunk)
        inner = dot(turned[g][0], k_ref[span, cols], NT)
        return inner, dot(turned[g][1], v_ref[span, cols], NT)

    def finish(g, c, inner, back, sums):
        cols, span = slice(g * size, (g + 1) * size), slice(c, c + chunk)
        rate = r_ref[pl.ds(first + g, 1), span]
        gate, up = inner[:size], inner[size:]
        back = back * rate
        sig = sigmoid(gate)
        silu = gate * sig
        hidden = (silu * (up * rate)).astype(jnp.bfloat16)
        gate_grad = (back * up * (sig + silu * (1.0 - sig))).astype(jnp.bfloat16)
        up_grad = (back * silu).astype(jnp.bfloat16)
        found = [
            dot(jnp.concatenate([gate_grad, up_grad], axis=0), k_ref[span, cols]),
            dot(hidden, v_ref[span, cols]),
        ]
        sums = found if sums is None else [a + b for a, b in zip(sums, found)]
        if c + chunk < rows:
            return sums
        total[g % 2, 0] = jnp.transpose(sums[0][:size])
        total[g % 2, 1] = jnp.transpose(sums[0][size:])
        total[g % 2, 2] = jnp.transpose(sums[1])
        for m in range(peers):
            row = pl.multiple_of((z_ref[0] ^ m) * own, own)
            outs[m][g] = total[g % 2, :, pl.ds(row, own), :].astype(outs[m].dtype)
        return None

    sums = None
    ready = products(*tasks[0])
    for i, task in enumerate(tasks):
        following = products(*tasks[i + 1]) if i + 1 < len(tasks) else None
        sums = finish(*task, *ready, sums)
        ready = following


def partial_grads(z, keys, values, rates, weights, peers, kinds):
    rows = keys.shape[0]
    heads, _, size, _ = weights.shape
    own = size // peers
    group = steps_of(heads)
    column = pl.BlockSpec((rows, group * size), lambda h, z: (0, h))
    return call(
        functools.partial(grad_body, peers, group, min(rows, 512)),
        (heads // group,),
        [
            column,
            column,
            pl.BlockSpec((heads, rows), lambda h, z: (0, 0)),
            pl.BlockSpec((group, 3, size, size), lambda h, z: (h, 0, 0, 0)),
        ],
        [pl.BlockSpec((group, 3, own, size), lambda h, z: (h, 0, 0, 0))] * peers,
        [jax.ShapeDtypeStruct((heads, 3, own, size), kind) for kind in kinds],
        [pltpu.VMEM((2, 3, size, size), jnp.float32)],
        1,
        12 * rows * heads * size * size,
        4 * rows * heads * size,
    )(z, far(keys), far(values), far(rates), far(weights))


def update_body(count, z_ref, w_ref, m_ref, *refs):
    terms, w_out, m_out = refs[:count], refs[count], refs[count + 1]
    for g in range(w_ref.shape[0]):
        new = momentum_keep * m_ref[g]
        for term in terms:
            new = new + term[g].astype(jnp.float32)
        before = w_ref[g].astype(jnp.float32)
        moved = before + new
        ratio = jnp.sqrt(
            (jnp.mean(before * before, axis=-1, keepdims=True) + epsilon)
            / (jnp.mean(moved * moved, axis=-1, keepdims=True) + epsilon)
        )
        m_out[g] = new
        w_out[g] = (moved * ratio).astype(w_out.dtype)


def updated(z, weights, momentum, terms):
    shape = momentum.shape
    whole = pl.BlockSpec(shape, lambda i, z: (0, 0, 0, 0))
    count = momentum.size
    return call(
        functools.partial(update_body, len(terms)),
        (1,),
        [pl.BlockSpec(shape, lambda i, z: (0, 0, z[0], 0)), whole] + [VMEM] * len(terms),
        [VMEM, whole],
        [jax.ShapeDtypeStruct(shape, jnp.bfloat16), jax.ShapeDtypeStruct(shape, jnp.float32)],
        (),
        1,
        20 * count,
        16 * count,
    )(z, weights, momentum, *terms)


def attend(tasks, s_ref):
    def scores(i):
        query, segments, _ = tasks[i]
        query = query()
        top = None
        for j, (key, _, mask) in enumerate(segments):
            score = dot(key(), query, NT)
            if mask is not None:
                score = jnp.where(mask, score, MASKED)
            s_ref[i % 2, j * TILE : (j + 1) * TILE, :] = score
            most = jnp.max(score.reshape(TILE // 8, 8, TILE), axis=0)
            top = most if top is None else jnp.maximum(top, most)
        return jnp.max(top, axis=0, keepdims=True)

    def weigh(i, top):
        _, segments, emit = tasks[i]
        factor = segments[0][0]().shape[1] ** (-0.5)
        out = total = None
        for j, (_, value, _) in enumerate(segments):
            score = s_ref[i % 2, j * TILE : (j + 1) * TILE, :]
            weight = jnp.exp2((score - top) * (factor * LOG2E))
            part = jnp.sum(weight.reshape(TILE // 8, 8, TILE), axis=0)
            product = dot(value(), weight.astype(jnp.bfloat16))
            total = part if total is None else total + part
            out = product if out is None else out + product
        total = jnp.sum(total, axis=0, keepdims=True)
        emit(out * (1.0 / total), top * factor + jnp.log(total))

    top = scores(0)
    for i in range(len(tasks)):
        following = scores(i + 1) if i + 1 < len(tasks) else None
        weigh(i, top)
        top = following


def masks():
    row = lax.broadcasted_iota(jnp.int32, (TILE, TILE), 0)
    col = lax.broadcasted_iota(jnp.int32, (TILE, TILE), 1)
    return row <= col, row > col


def spans(ref, t, cols):
    return lambda: ref[t * TILE : (t + 1) * TILE, cols]


def turned(memo, ref, t, cols, key):
    def load():
        if (key, t) not in memo:
            memo[key, t] = jnp.transpose(ref[t * TILE : (t + 1) * TILE, cols])
        return memo[key, t]

    return load


def put(o_ref, t, cols):
    def emit(out, level):
        o_ref[t * TILE : (t + 1) * TILE, cols] = jnp.transpose(out).astype(o_ref.dtype)

    return emit


SCORES = (WIN // TILE + 1) * TILE


def later_body(group, q_ref, k_ref, v_ref, *refs):
    o_ref, s_ref = refs[-2:]
    size = q_ref.shape[1] // group
    causal, late = masks()
    depth = WIN // TILE
    tasks = []
    for g in range(group):
        cols = slice(g * size, (g + 1) * size)
        memo = {}
        for t in range(depth, q_ref.shape[0] // TILE):
            found = [
                (
                    spans(k_ref, j, cols),
                    turned(memo, v_ref, j, cols, 0),
                    causal if j == t else late if j == t - depth else None,
                )
                for j in range(t - depth, t + 1)
            ]
            tasks.append((spans(q_ref, t, cols), found, put(o_ref, t - depth, cols)))
    attend(tasks, s_ref)


def later_blocks(queries, keys, values, size, step, group, partly):
    rows, width = queries.shape
    column = pl.BlockSpec((rows, group * size), lambda h: (0, step))
    more = [] if partly is None else [partly]
    return pl.pallas_call(
        functools.partial(later_body, group),
        name="later",
        out_shape=jax.ShapeDtypeStruct((rows - WIN, width), jnp.bfloat16),
        grid_spec=pltpu.PrefetchScalarGridSpec(
            num_scalar_prefetch=0,
            grid=(1,),
            in_specs=[column] * 3 + [pl.BlockSpec(memory_space=pl.ANY)] * len(more),
            out_specs=pl.BlockSpec((rows - WIN, group * size), lambda h: (0, step)),
            scratch_shapes=[pltpu.VMEM((2, SCORES, TILE), jnp.float32)],
        ),
        compiler_params=PARAMS,
        input_output_aliases={3: 0} if more else {},
        cost_estimate=pl.CostEstimate(
            flops=6 * (rows - WIN) * WIN * size * group,
            bytes_accessed=8 * rows * size * group,
            transcendentals=0,
        ),
    )(queries, keys, values, *more)


def carried_body(group, z_ref, q_ref, k_ref, v_ref, p_ref, o_ref, s_ref):
    size = q_ref.shape[1] // group
    causal, late = masks()
    depth = WIN // TILE
    there = jnp.broadcast_to(z_ref[0] > 0, causal.shape)
    tasks = []
    for g in range(group):
        cols = slice(g * size, (g + 1) * size)
        memo = {}
        for t in range(depth):
            found = [
                (spans(p_ref.at[0], j, cols), turned(memo, p_ref.at[1], j, cols, 1), late & there if j == t else there)
                for j in range(t, depth)
            ]
            found += [
                (spans(k_ref, j, cols), turned(memo, v_ref, j, cols, 0), causal if j == t else None)
                for j in range(t + 1)
            ]
            tasks.append((spans(q_ref, t, cols), found, put(o_ref, t, cols)))
    attend(tasks, s_ref)


def carried_block(z, queries, keys, values, carried, size):
    heads = carried.shape[2] // size
    group = heads
    width = queries.shape[1]
    column = pl.BlockSpec((WIN, group * size), lambda h, z: (0, h))
    return call(
        functools.partial(carried_body, group),
        (heads // group,),
        [column] * 3 + [VMEM],
        column,
        jax.ShapeDtypeStruct((WIN, width), jnp.bfloat16),
        [pltpu.VMEM((2, SCORES, TILE), jnp.float32)],
        1,
        6 * WIN * WIN * size * heads,
        10 * WIN * size * heads,
    )(z, queries, keys, values, carried)


EXTRA = 16
KEPT = 3


def put_partial(o_ref, g, t, size):
    def emit(out, level):
        span = slice(t * TILE, (t + 1) * TILE)
        o_ref[g, :size, span] = out.astype(o_ref.dtype)
        rest, parts = level, []
        for _ in range(3):
            term = rest.astype(jnp.bfloat16).astype(jnp.float32)
            parts.append(term)
            rest = rest - term
        parts.append(jnp.zeros((EXTRA - 3, TILE), jnp.float32))
        o_ref[g, size:, span] = jnp.concatenate(parts, axis=0).astype(o_ref.dtype)

    return emit


def next_part_body(group, q_ref, k_ref, v_ref, o_ref, s_ref):
    size = q_ref.shape[1] // group
    _, late = masks()
    depth = WIN // TILE
    tasks = []
    for g in range(group):
        cols = slice(g * size, (g + 1) * size)
        memo = {}
        for t in range(depth):
            found = [
                (spans(k_ref, j, cols), turned(memo, v_ref, j, cols, 0), late if j == t else None)
                for j in range(t, depth)
            ]
            tasks.append((spans(q_ref, t, cols), found, put_partial(o_ref, g, t, size)))
    attend(tasks, s_ref)


def next_part(asked, keys, values, first, size):
    heads = asked.shape[1] // size
    block = keys.shape[0] // WIN - 1
    group = math.gcd(heads, first)
    column = pl.BlockSpec((WIN, group * size), lambda h: (block, h + first // group))
    return call(
        functools.partial(next_part_body, group),
        (heads // group,),
        [pl.BlockSpec((WIN, group * size), lambda h: (0, h)), column, column],
        pl.BlockSpec((group, size + EXTRA, WIN), lambda h: (h, 0, 0)),
        jax.ShapeDtypeStruct((heads, size + EXTRA, WIN), jnp.bfloat16),
        [pltpu.VMEM((2, WIN, TILE), jnp.float32)],
        0,
        4 * WIN * WIN * size * heads,
        8 * WIN * size * heads,
    )(asked, keys, values)


def joined_body(group, z_ref, q_ref, k_ref, v_ref, p_ref, _, o_ref, s_ref):
    size = q_ref.shape[1] // group
    causal, _ = masks()
    depth = WIN // TILE
    step = pl.program_id(0) * group

    def join(g, t, cols):
        def emit(out, level):
            span = slice(t * TILE, (t + 1) * TILE)
            terms = p_ref[step + g, size:, span].astype(jnp.float32)
            other = terms[0:1] + (terms[1:2] + terms[2:3])
            share = jnp.where(z_ref[0] > 0, jax.nn.sigmoid(other - level), 0.0)
            out = out + share * (p_ref[step + g, :size, span].astype(jnp.float32) - out)
            o_ref[span, cols] = jnp.transpose(out).astype(o_ref.dtype)

        return emit

    tasks = []
    for g in range(group):
        cols = slice(g * size, (g + 1) * size)
        memo = {}
        for t in range(depth):
            found = [
                (spans(k_ref, j, cols), turned(memo, v_ref, j, cols, 0), causal if j == t else None)
                for j in range(t + 1)
            ]
            tasks.append((spans(q_ref, t, cols), found, join(g, t, cols)))
    attend(tasks, s_ref)


def joined_block(z, queries, keys, values, given, partly, first, size):
    heads = given.shape[0]
    group = math.gcd(heads, first)
    column = pl.BlockSpec((WIN, group * size), lambda h, z: (0, h + first // group))
    return pl.pallas_call(
        functools.partial(joined_body, group),
        name="joined",
        out_shape=jax.ShapeDtypeStruct(partly.shape, partly.dtype),
        grid_spec=pltpu.PrefetchScalarGridSpec(
            num_scalar_prefetch=1,
            grid=(heads // group,),
            in_specs=[
                column,
                column,
                column,
                VMEM,
                pl.BlockSpec(memory_space=pl.ANY),
            ],
            out_specs=column,
            scratch_shapes=[pltpu.VMEM((2, WIN, TILE), jnp.float32)],
        ),
        compiler_params=PARAMS,
        input_output_aliases={5: 0},
        cost_estimate=pl.CostEstimate(
            flops=4 * WIN * WIN * size * heads, bytes_accessed=10 * WIN * size * heads, transcendentals=0
        ),
    )(z, queries, keys, values, given, partly)


def final_body(peers, group, z_ref, q_ref, first_ref, later_ref, *refs):
    blocks, o_ref, whole = refs[:peers], refs[peers], refs[peers + 1]
    size = q_ref.shape[1] // group
    own = blocks[0].shape[2]
    start = pl.program_id(0) * group
    for m in range(peers):
        row = pl.multiple_of((z_ref[0] ^ m) * own, own)
        whole[:, :, pl.ds(row, own), :] = blocks[m][pl.ds(start, group)].astype(whole.dtype)
    tasks = [(g, c) for g in range(group) for c in range(0, q_ref.shape[0], WIN)]

    def products(g, c):
        query = q_ref[c : c + WIN, g * size : (g + 1) * size]
        both = jnp.concatenate([whole[g, 0], whole[g, 1]], axis=1).astype(jnp.bfloat16)
        return dot(query, both)

    def finish(g, c, inner):
        cols = slice(g * size, (g + 1) * size)
        gate, up = inner[:, :size], inner[:, size:]
        hidden = (gate * sigmoid(gate) * up).astype(jnp.bfloat16)
        fast = dot(hidden, whole[g, 2].astype(jnp.bfloat16), NT)
        kept = first_ref[:, cols] if c == 0 else later_ref[c - WIN : c, cols]
        o_ref[c : c + WIN, cols] = (fast + kept.astype(jnp.float32)).astype(o_ref.dtype)

    ready = products(*tasks[0])
    for i, task in enumerate(tasks):
        following = products(*tasks[i + 1]) if i + 1 < len(tasks) else None
        finish(*task, ready)
        ready = following


def final(z, queries, first, later, blocks, size):
    rows, width = queries.shape
    heads = width // size
    group = steps_of(heads)
    peers, own = len(blocks), blocks[0].shape[2]
    column = pl.BlockSpec((rows, group * size), lambda h, z: (0, h))
    kind = jnp.bfloat16 if own % 16 == 0 else jnp.float32
    return call(
        functools.partial(final_body, peers, group),
        (heads // group,),
        [
            column,
            pl.BlockSpec((WIN, group * size), lambda h, z: (0, h)),
            pl.BlockSpec((rows - WIN, group * size), lambda h, z: (0, h)),
        ]
        + [VMEM] * peers,
        column,
        jax.ShapeDtypeStruct((rows, width), jnp.bfloat16),
        [pltpu.VMEM((group, 3, size, size), kind)],
        1,
        6 * rows * width * size,
        6 * rows * width,
    )(z, queries, first, later, *blocks)


def pack_body(cut, q_ref, k_ref, v_ref, ask_ref, carry_ref, sems):
    rows = q_ref.shape[0]
    tail = pl.ds(rows - WIN, WIN)
    copies = [
        pltpu.make_async_copy(
            q_ref.at[pl.ds(0, WIN), pl.ds(cut, q_ref.shape[1] - cut)], ask_ref, sems.at[0]
        ),
        pltpu.make_async_copy(k_ref.at[tail, pl.ds(0, cut)], carry_ref.at[0], sems.at[1]),
        pltpu.make_async_copy(v_ref.at[tail, pl.ds(0, cut)], carry_ref.at[1], sems.at[2]),
    ]
    for copy in copies:
        copy.start()
    for copy in copies:
        copy.wait()


def packed(queries, keys, values, cut):
    width = queries.shape[1]
    here = pl.BlockSpec(memory_space=pltpu.HBM)
    return call(
        functools.partial(pack_body, cut),
        (),
        [here] * 3,
        [VMEM] * 2,
        [
            jax.ShapeDtypeStruct((WIN, width - cut), queries.dtype),
            jax.ShapeDtypeStruct((2, WIN, cut), keys.dtype),
        ],
        [pltpu.SemaphoreType.DMA((3,))],
        0,
        0,
        4 * WIN * (width + cut),
    )(far(queries), far(keys), far(values))


def moved_by(value, by):
    peers = lax.axis_size("seq")
    pairs = [(i, i + by) for i in range(peers) if 0 <= i + by < peers]
    return lax.ppermute(value, "seq", pairs)


def swapped(value, mask):
    return lax.ppermute(value, "seq", [(i, i ^ mask) for i in range(lax.axis_size("seq"))])


def kept_of(heads):
    return max(1, heads * KEPT // 10)


def shards(queries, keys, values, rates, fast_weights, momentum):
    heads = rates.shape[0]
    size = fast_weights.shape[0]
    peers = lax.axis_size("seq")
    kept = kept_of(heads)
    z = lax.axis_index("seq").astype(jnp.int32).reshape(1)
    cut = kept * size

    asked, carried = packed(queries, keys, values, cut)
    asked = moved_by(asked, -1)
    carried = moved_by(carried, 1)

    weights = jnp.transpose(fast_weights, (1, 2, 0, 3))
    own_momentum = jnp.transpose(momentum, (1, 2, 0, 3))
    kinds = [jnp.bfloat16 if m % 2 else jnp.float32 for m in range(peers)]
    sums = [[block] for block in partial_grads(z, keys, values, rates, weights, peers, kinds)]

    step = 1
    while step < peers:
        for m in reversed(range(peers)):
            if m % (2 * step) == step:
                terms = sums[m]
                block = functools.reduce(jnp.add, [t.astype(jnp.float32) for t in terms])
                sums[m - step].append(swapped(block.astype(jnp.bfloat16), step))
        step *= 2

    group = steps_of(heads)
    later = None
    for part in range(heads // group):
        later = later_blocks(queries, keys, values, size, part, group, later)
    given = next_part(asked, keys, values, kept, size)
    given = moved_by(given, 1)
    first = carried_block(z, queries, keys, values, carried, size)
    first = joined_block(z, queries, keys, values, given, first, kept, size)

    new_rows, new_momentum = updated(z, weights, own_momentum, sums[0])
    blocks = {0: new_rows}
    step = peers // 2
    while step:
        for m in sorted(blocks):
            blocks[m + step] = swapped(blocks[m], step)
        step //= 2
    blocks = [blocks[m] for m in range(peers)]

    mixed = final(z, queries, first, later, blocks, size)
    return (mixed, jnp.transpose(new_rows, (2, 0, 1, 3)), jnp.transpose(new_momentum, (2, 0, 1, 3)))


def solution(mesh):
    return jax.shard_map(
        shards,
        mesh=mesh,
        in_specs=(
            P(("groups", "seq"), ("head", "rep")),
            P(("groups", "seq"), ("head", "rep")),
            P(("groups", "seq"), ("head", "rep")),
            P(("head", "rep"), ("groups", "seq")),
            P(None, ("head", "rep"), None, None),
            P("seq", ("head", "rep"), None, None),
        ),
        out_specs=(
            P(("groups", "seq"), ("head", "rep")),
            P(("groups", "seq"), ("head", "rep"), None, None),
            P(("groups", "seq"), ("head", "rep"), None, None),
        ),
        check_vma=False,
    )
```

```python
import functools
import math

import jax
import jax.numpy as jnp
from jax import lax
from jax.experimental import pallas as pl
from jax.experimental.pallas import tpu as pltpu
from jax.sharding import PartitionSpec as P


WIN = 512
TILE = 256

momentum_keep = 0.9
epsilon = 1e-06
MASKED = -1e30
LOG2E = math.log2(math.e)
PARAMS = pltpu.CompilerParams(vmem_limit_bytes=24 * 2**20)
VMEM = pl.BlockSpec(memory_space=pltpu.VMEM)
NT = (((1,), (1,)), ((), ()))


def call(body, grid, in_specs, out_specs, out_shape, scratch=(), prefetch=0, flops=0, nbytes=0):
    return pl.pallas_call(
        body,
        out_shape=out_shape,
        grid_spec=pltpu.PrefetchScalarGridSpec(
            num_scalar_prefetch=prefetch,
            grid=grid,
            in_specs=in_specs,
            out_specs=out_specs,
            scratch_shapes=list(scratch),
        ),
        compiler_params=PARAMS,
        cost_estimate=pl.CostEstimate(flops=flops, bytes_accessed=nbytes, transcendentals=0),
    )


def far(x):
    return pltpu.with_memory_space_constraint(x, pltpu.HBM)


def sigmoid(x):
    return 0.5 * jnp.tanh(0.5 * x) + 0.5


def dot(a, b, dims=None):
    if dims is None:
        return jnp.dot(a, b, preferred_element_type=jnp.float32)
    return lax.dot_general(a, b, dims, preferred_element_type=jnp.float32)


def steps_of(heads, most=5):
    return next(n for n in range(min(heads, most), 0, -1) if heads % n == 0)


def grad_body(peers, group, chunk, z_ref, k_ref, v_ref, r_ref, w_ref, *refs):
    outs, total = refs[:peers], refs[peers]
    size = w_ref.shape[2]
    rows = k_ref.shape[0]
    own = outs[0].shape[2]
    first = pl.program_id(0) * group
    tasks = [(g, c) for g in range(group) for c in range(0, rows, chunk)]
    turned = {}

    def products(g, c):
        if g not in turned:
            flipped = [jnp.transpose(w_ref[g, m]) for m in range(3)]
            turned[g] = (jnp.concatenate(flipped[:2], axis=0), flipped[2])
        cols, span = slice(g * size, (g + 1) * size), slice(c, c + chunk)
        inner = dot(turned[g][0], k_ref[span, cols], NT)
        return inner, dot(turned[g][1], v_ref[span, cols], NT)

    def finish(g, c, inner, back, sums):
        cols, span = slice(g * size, (g + 1) * size), slice(c, c + chunk)
        rate = r_ref[pl.ds(first + g, 1), span]
        gate, up = inner[:size], inner[size:]
        back = back * rate
        sig = sigmoid(gate)
        silu = gate * sig
        hidden = (silu * (up * rate)).astype(jnp.bfloat16)
        gate_grad = (back * up * (sig + silu * (1.0 - sig))).astype(jnp.bfloat16)
        up_grad = (back * silu).astype(jnp.bfloat16)
        found = [
            dot(jnp.concatenate([gate_grad, up_grad], axis=0), k_ref[span, cols]),
            dot(hidden, v_ref[span, cols]),
        ]
        sums = found if sums is None else [a + b for a, b in zip(sums, found)]
        if c + chunk < rows:
            return sums
        total[g % 2, 0] = jnp.transpose(sums[0][:size])
        total[g % 2, 1] = jnp.transpose(sums[0][size:])
        total[g % 2, 2] = jnp.transpose(sums[1])
        for m in range(peers):
            row = pl.multiple_of((z_ref[0] ^ m) * own, own)
            outs[m][g] = total[g % 2, :, pl.ds(row, own), :].astype(outs[m].dtype)
        return None

    sums = None
    ready = products(*tasks[0])
    for i, task in enumerate(tasks):
        following = products(*tasks[i + 1]) if i + 1 < len(tasks) else None
        sums = finish(*task, *ready, sums)
        ready = following


def partial_grads(z, keys, values, rates, weights, peers, kinds):
    rows = keys.shape[0]
    heads, _, size, _ = weights.shape
    own = size // peers
    group = steps_of(heads)
    column = pl.BlockSpec((rows, group * size), lambda h, z: (0, h))
    return call(
        functools.partial(grad_body, peers, group, min(rows, 512)),
        (heads // group,),
        [
            column,
            column,
            pl.BlockSpec((heads, rows), lambda h, z: (0, 0)),
            pl.BlockSpec((group, 3, size, size), lambda h, z: (h, 0, 0, 0)),
        ],
        [pl.BlockSpec((group, 3, own, size), lambda h, z: (h, 0, 0, 0))] * peers,
        [jax.ShapeDtypeStruct((heads, 3, own, size), kind) for kind in kinds],
        [pltpu.VMEM((2, 3, size, size), jnp.float32)],
        1,
        12 * rows * heads * size * size,
        4 * rows * heads * size,
    )(z, keys, far(values), far(rates), far(weights))


def update_body(count, z_ref, w_ref, m_ref, *refs):
    terms, w_out, m_out = refs[:count], refs[count], refs[count + 1]
    for g in range(w_ref.shape[0]):
        new = momentum_keep * m_ref[g]
        for term in terms:
            new = new + term[g].astype(jnp.float32)
        before = w_ref[g].astype(jnp.float32)
        moved = before + new
        ratio = jnp.sqrt(
            (jnp.mean(before * before, axis=-1, keepdims=True) + epsilon)
            / (jnp.mean(moved * moved, axis=-1, keepdims=True) + epsilon)
        )
        m_out[g] = new
        w_out[g] = (moved * ratio).astype(w_out.dtype)


def updated(z, weights, momentum, terms):
    shape = momentum.shape
    whole = pl.BlockSpec(shape, lambda i, z: (0, 0, 0, 0))
    count = momentum.size
    return call(
        functools.partial(update_body, len(terms)),
        (1,),
        [pl.BlockSpec(shape, lambda i, z: (0, 0, z[0], 0)), whole] + [VMEM] * len(terms),
        [VMEM, whole],
        [jax.ShapeDtypeStruct(shape, jnp.bfloat16), jax.ShapeDtypeStruct(shape, jnp.float32)],
        (),
        1,
        20 * count,
        16 * count,
    )(z, weights, momentum, *terms)


def attend(tasks, s_ref):
    def scores(i):
        query, segments, _ = tasks[i]
        query = query()
        top = None
        for j, (key, _, mask) in enumerate(segments):
            score = dot(key(), query, NT)
            if mask is not None:
                score = jnp.where(mask, score, MASKED)
            s_ref[i % 2, j * TILE : (j + 1) * TILE, :] = score
            most = jnp.max(score.reshape(TILE // 8, 8, TILE), axis=0)
            top = most if top is None else jnp.maximum(top, most)
        return jnp.max(top, axis=0, keepdims=True)

    def weigh(i, top):
        _, segments, emit = tasks[i]
        factor = segments[0][0]().shape[1] ** (-0.5)
        out = total = None
        for j, (_, value, _) in enumerate(segments):
            score = s_ref[i % 2, j * TILE : (j + 1) * TILE, :]
            weight = jnp.exp2((score - top) * (factor * LOG2E))
            part = jnp.sum(weight.reshape(TILE // 8, 8, TILE), axis=0)
            product = dot(value(), weight.astype(jnp.bfloat16))
            total = part if total is None else total + part
            out = product if out is None else out + product
        total = jnp.sum(total, axis=0, keepdims=True)
        emit(out * (1.0 / total), top * factor + jnp.log(total))

    top = scores(0)
    for i in range(len(tasks)):
        following = scores(i + 1) if i + 1 < len(tasks) else None
        weigh(i, top)
        top = following


def masks():
    row = lax.broadcasted_iota(jnp.int32, (TILE, TILE), 0)
    col = lax.broadcasted_iota(jnp.int32, (TILE, TILE), 1)
    return row <= col, row > col


def spans(ref, t, cols):
    return lambda: ref[t * TILE : (t + 1) * TILE, cols]


def turned(memo, ref, t, cols, key):
    def load():
        if (key, t) not in memo:
            memo[key, t] = jnp.transpose(ref[t * TILE : (t + 1) * TILE, cols])
        return memo[key, t]

    return load


def put(o_ref, t, cols):
    def emit(out, level):
        o_ref[t * TILE : (t + 1) * TILE, cols] = jnp.transpose(out).astype(o_ref.dtype)

    return emit


SCORES = (WIN // TILE + 1) * TILE


def later_body(group, q_ref, k_ref, v_ref, *refs):
    o_ref, s_ref = refs[-2:]
    size = q_ref.shape[1] // group
    causal, late = masks()
    depth = WIN // TILE
    tasks = []
    for g in range(group):
        cols = slice(g * size, (g + 1) * size)
        memo = {}
        for t in range(depth, q_ref.shape[0] // TILE):
            found = [
                (
                    spans(k_ref, j, cols),
                    turned(memo, v_ref, j, cols, 0),
                    causal if j == t else late if j == t - depth else None,
                )
                for j in range(t - depth, t + 1)
            ]
            tasks.append((spans(q_ref, t, cols), found, put(o_ref, t - depth, cols)))
    attend(tasks, s_ref)


def later_blocks(queries, keys, values, size, step, group, partly):
    rows, width = queries.shape
    column = pl.BlockSpec((rows, group * size), lambda h: (0, step))
    more = [] if partly is None else [partly]
    return pl.pallas_call(
        functools.partial(later_body, group),
        name="later",
        out_shape=jax.ShapeDtypeStruct((rows - WIN, width), jnp.bfloat16),
        grid_spec=pltpu.PrefetchScalarGridSpec(
            num_scalar_prefetch=0,
            grid=(1,),
            in_specs=[column] * 3 + [pl.BlockSpec(memory_space=pl.ANY)] * len(more),
            out_specs=pl.BlockSpec((rows - WIN, group * size), lambda h: (0, step)),
            scratch_shapes=[pltpu.VMEM((2, SCORES, TILE), jnp.float32)],
        ),
        compiler_params=PARAMS,
        input_output_aliases={3: 0} if more else {},
        cost_estimate=pl.CostEstimate(
            flops=6 * (rows - WIN) * WIN * size * group,
            bytes_accessed=8 * rows * size * group,
            transcendentals=0,
        ),
    )(queries, keys, values, *more)


def carried_body(group, z_ref, q_ref, k_ref, v_ref, p_ref, o_ref, s_ref):
    size = q_ref.shape[1] // group
    causal, late = masks()
    depth = WIN // TILE
    there = jnp.broadcast_to(z_ref[0] > 0, causal.shape)
    tasks = []
    for g in range(group):
        cols = slice(g * size, (g + 1) * size)
        memo = {}
        for t in range(depth):
            found = [
                (spans(p_ref.at[0], j, cols), turned(memo, p_ref.at[1], j, cols, 1), late & there if j == t else there)
                for j in range(t, depth)
            ]
            found += [
                (spans(k_ref, j, cols), turned(memo, v_ref, j, cols, 0), causal if j == t else None)
                for j in range(t + 1)
            ]
            tasks.append((spans(q_ref, t, cols), found, put(o_ref, t, cols)))
    attend(tasks, s_ref)


def carried_block(z, queries, keys, values, carried, size):
    heads = carried.shape[2] // size
    group = heads
    width = queries.shape[1]
    column = pl.BlockSpec((WIN, group * size), lambda h, z: (0, h))
    return call(
        functools.partial(carried_body, group),
        (heads // group,),
        [column] * 3 + [VMEM],
        column,
        jax.ShapeDtypeStruct((WIN, width), jnp.bfloat16),
        [pltpu.VMEM((2, SCORES, TILE), jnp.float32)],
        1,
        6 * WIN * WIN * size * heads,
        10 * WIN * size * heads,
    )(z, queries, keys, values, carried)


EXTRA = 8
KEPT = 3
EARLY = 4


def put_partial(o_ref, g, t, size):
    def emit(out, level):
        span = slice(t * TILE, (t + 1) * TILE)
        o_ref[g, :size, span] = out.astype(o_ref.dtype)
        rest, parts = level, []
        for _ in range(3):
            term = rest.astype(jnp.bfloat16).astype(jnp.float32)
            parts.append(term)
            rest = rest - term
        parts.append(jnp.zeros((EXTRA - 3, TILE), jnp.float32))
        o_ref[g, size:, span] = jnp.concatenate(parts, axis=0).astype(o_ref.dtype)

    return emit


def next_part_body(group, q_ref, k_ref, v_ref, o_ref, s_ref):
    size = q_ref.shape[1] // group
    _, late = masks()
    depth = WIN // TILE
    tasks = []
    for g in range(group):
        cols = slice(g * size, (g + 1) * size)
        memo = {}
        for t in range(depth):
            found = [
                (spans(k_ref, j, cols), turned(memo, v_ref, j, cols, 0), late if j == t else None)
                for j in range(t, depth)
            ]
            tasks.append((spans(q_ref, t, cols), found, put_partial(o_ref, g, t, size)))
    attend(tasks, s_ref)


def next_part(asked, keys, values, first, size):
    heads = asked.shape[1] // size
    block = keys.shape[0] // WIN - 1
    group = math.gcd(heads, first)
    column = pl.BlockSpec((WIN, group * size), lambda h: (block, h + first // group))
    return call(
        functools.partial(next_part_body, group),
        (heads // group,),
        [pl.BlockSpec((WIN, group * size), lambda h: (0, h)), column, column],
        pl.BlockSpec((group, size + EXTRA, WIN), lambda h: (h, 0, 0)),
        jax.ShapeDtypeStruct((heads, size + EXTRA, WIN), jnp.bfloat16),
        [pltpu.VMEM((2, WIN, TILE), jnp.float32)],
        0,
        4 * WIN * WIN * size * heads,
        8 * WIN * size * heads,
    )(asked, keys, values)


def joined_body(group, z_ref, q_ref, k_ref, v_ref, p_ref, _, o_ref, s_ref):
    size = q_ref.shape[1] // group
    causal, _ = masks()
    depth = WIN // TILE
    step = pl.program_id(0) * group

    def join(g, t, cols):
        def emit(out, level):
            span = slice(t * TILE, (t + 1) * TILE)
            terms = p_ref[step + g, size:, span].astype(jnp.float32)
            other = terms[0:1] + (terms[1:2] + terms[2:3])
            share = jnp.where(z_ref[0] > 0, jax.nn.sigmoid(other - level), 0.0)
            out = out + share * (p_ref[step + g, :size, span].astype(jnp.float32) - out)
            o_ref[span, cols] = jnp.transpose(out).astype(o_ref.dtype)

        return emit

    tasks = []
    for g in range(group):
        cols = slice(g * size, (g + 1) * size)
        memo = {}
        for t in range(depth):
            found = [
                (spans(k_ref, j, cols), turned(memo, v_ref, j, cols, 0), causal if j == t else None)
                for j in range(t + 1)
            ]
            tasks.append((spans(q_ref, t, cols), found, join(g, t, cols)))
    attend(tasks, s_ref)


def joined_block(z, queries, keys, values, given, partly, first, size):
    heads = given.shape[0]
    group = math.gcd(heads, first)
    column = pl.BlockSpec((WIN, group * size), lambda h, z: (0, h + first // group))
    return pl.pallas_call(
        functools.partial(joined_body, group),
        name="joined",
        out_shape=jax.ShapeDtypeStruct(partly.shape, partly.dtype),
        grid_spec=pltpu.PrefetchScalarGridSpec(
            num_scalar_prefetch=1,
            grid=(heads // group,),
            in_specs=[
                column,
                column,
                column,
                VMEM,
                pl.BlockSpec(memory_space=pl.ANY),
            ],
            out_specs=column,
            scratch_shapes=[pltpu.VMEM((2, WIN, TILE), jnp.float32)],
        ),
        compiler_params=PARAMS,
        input_output_aliases={5: 0},
        cost_estimate=pl.CostEstimate(
            flops=4 * WIN * WIN * size * heads, bytes_accessed=10 * WIN * size * heads, transcendentals=0
        ),
    )(z, queries, keys, values, given, partly)


def final_body(peers, group, z_ref, q_ref, first_ref, later_ref, *refs):
    blocks, o_ref, whole = refs[:peers], refs[peers], refs[peers + 1]
    size = q_ref.shape[1] // group
    own = blocks[0].shape[2]
    start = pl.program_id(0) * group
    for m in range(peers):
        row = pl.multiple_of((z_ref[0] ^ m) * own, own)
        whole[:, :, pl.ds(row, own), :] = blocks[m][pl.ds(start, group)].astype(whole.dtype)
    tasks = [(g, c) for g in range(group) for c in range(0, q_ref.shape[0], WIN)]

    def products(g, c):
        query = q_ref[c : c + WIN, g * size : (g + 1) * size]
        both = jnp.concatenate([whole[g, 0], whole[g, 1]], axis=1).astype(jnp.bfloat16)
        return dot(query, both)

    def finish(g, c, inner):
        cols = slice(g * size, (g + 1) * size)
        gate, up = inner[:, :size], inner[:, size:]
        hidden = (gate * sigmoid(gate) * up).astype(jnp.bfloat16)
        fast = dot(hidden, whole[g, 2].astype(jnp.bfloat16), NT)
        kept = first_ref[:, cols] if c == 0 else later_ref[c - WIN : c, cols]
        o_ref[c : c + WIN, cols] = (fast + kept.astype(jnp.float32)).astype(o_ref.dtype)

    ready = products(*tasks[0])
    for i, task in enumerate(tasks):
        following = products(*tasks[i + 1]) if i + 1 < len(tasks) else None
        finish(*task, ready)
        ready = following


def final(z, queries, first, later, blocks, size):
    rows, width = queries.shape
    heads = width // size
    group = steps_of(heads)
    peers, own = len(blocks), blocks[0].shape[2]
    column = pl.BlockSpec((rows, group * size), lambda h, z: (0, h))
    kind = jnp.bfloat16 if own % 16 == 0 else jnp.float32
    return call(
        functools.partial(final_body, peers, group),
        (heads // group,),
        [
            column,
            pl.BlockSpec((WIN, group * size), lambda h, z: (0, h)),
            pl.BlockSpec((rows - WIN, group * size), lambda h, z: (0, h)),
        ]
        + [VMEM] * peers,
        column,
        jax.ShapeDtypeStruct((rows, width), jnp.bfloat16),
        [pltpu.VMEM((group, 3, size, size), kind)],
        1,
        6 * rows * width * size,
        6 * rows * width,
    )(z, queries, first, later, *blocks)


def pack_body(first, q_ref, k_ref, v_ref, ask_ref, carry_ref, sems):
    cut = carry_ref.shape[2]
    tail = pl.ds(q_ref.shape[0] - WIN, WIN)
    copies = [
        (k_ref.at[tail, pl.ds(0, cut)], carry_ref.at[0]),
        (v_ref.at[tail, pl.ds(0, cut)], carry_ref.at[1]),
        (q_ref.at[pl.ds(0, WIN), pl.ds(first, ask_ref.shape[1])], ask_ref),
    ]
    copies = [pltpu.make_async_copy(*c, sems.at[i]) for i, c in enumerate(copies)]
    for copy in copies:
        copy.start()
    for copy in copies:
        copy.wait()


def packed(queries, keys, values, cut, asked):
    here = pl.BlockSpec(memory_space=pltpu.HBM)
    shapes = [(WIN, asked[1]), (2, WIN, cut)]
    return call(
        functools.partial(pack_body, asked[0]),
        (),
        [here] * 3,
        [VMEM] * 2,
        [jax.ShapeDtypeStruct(shape, queries.dtype) for shape in shapes],
        [pltpu.SemaphoreType.DMA((3,))],
        0,
        0,
        4 * WIN * (2 * cut + asked[1]),
    )(far(queries), far(keys), far(values))


def moved_by(value, by):
    peers = lax.axis_size("seq")
    pairs = [(i, i + by) for i in range(peers) if 0 <= i + by < peers]
    return lax.ppermute(value, "seq", pairs)


def swapped(value, mask):
    return lax.ppermute(value, "seq", [(i, i ^ mask) for i in range(lax.axis_size("seq"))])


def kept_of(heads):
    return max(1, heads * KEPT // 10)


def shards(queries, keys, values, rates, fast_weights, momentum):
    heads = rates.shape[0]
    size = fast_weights.shape[0]
    peers = lax.axis_size("seq")
    kept = kept_of(heads)
    z = lax.axis_index("seq").astype(jnp.int32).reshape(1)
    early = max(1, heads * EARLY // 10)
    groups = [(kept, early), (kept + early, heads - kept - early)]

    asked, carried = packed(queries, keys, values, kept * size, (kept * size, early * size))
    asked = [moved_by(asked, -1)]
    asked.append(moved_by(queries[:WIN, (kept + early) * size :], -1))
    carried = moved_by(carried, 1)

    weights = jnp.transpose(fast_weights, (1, 2, 0, 3))
    own_momentum = jnp.transpose(momentum, (1, 2, 0, 3))
    kinds = [jnp.bfloat16 if m % 2 else jnp.float32 for m in range(peers)]
    sums = [[block] for block in partial_grads(z, keys, values, rates, weights, peers, kinds)]

    step = 1
    while step < peers:
        for m in reversed(range(peers)):
            if m % (2 * step) == step:
                terms = sums[m]
                block = functools.reduce(jnp.add, [t.astype(jnp.float32) for t in terms])
                sums[m - step].append(swapped(block.astype(jnp.bfloat16), step))
        step *= 2

    group = steps_of(heads)
    later = None
    for part in range(heads // group):
        later = later_blocks(queries, keys, values, size, part, group, later)
    given = []
    for i, (place, _) in enumerate(groups):
        part = next_part(asked[i], keys, values, place, size)
        given.append(moved_by(part, 1))
    first = carried_block(z, queries, keys, values, carried, size)
    for i, (place, _) in enumerate(groups):
        first = joined_block(z, queries, keys, values, given[i], first, place, size)

    new_rows, new_momentum = updated(z, weights, own_momentum, sums[0])
    blocks = {0: new_rows}
    step = peers // 2
    while step:
        for m in sorted(blocks):
            blocks[m + step] = swapped(blocks[m], step)
        step //= 2
    blocks = [blocks[m] for m in range(peers)]

    mixed = final(z, queries, first, later, blocks, size)
    return (mixed, jnp.transpose(new_rows, (2, 0, 1, 3)), jnp.transpose(new_momentum, (2, 0, 1, 3)))


def solution(mesh):
    return jax.shard_map(
        shards,
        mesh=mesh,
        in_specs=(
            P(("groups", "seq"), ("head", "rep")),
            P(("groups", "seq"), ("head", "rep")),
            P(("groups", "seq"), ("head", "rep")),
            P(("head", "rep"), ("groups", "seq")),
            P(None, ("head", "rep"), None, None),
            P("seq", ("head", "rep"), None, None),
        ),
        out_specs=(
            P(("groups", "seq"), ("head", "rep")),
            P(("groups", "seq"), ("head", "rep"), None, None),
            P(("groups", "seq"), ("head", "rep"), None, None),
        ),
        check_vma=False,
    )
```

```python
import functools
import math

import jax
import jax.numpy as jnp
from jax import lax
from jax.experimental import pallas as pl
from jax.experimental.pallas import tpu as pltpu
from jax.sharding import PartitionSpec as P


WIN = 512
TILE = 256

momentum_keep = 0.9
epsilon = 1e-06
MASKED = -1e30
LOG2E = math.log2(math.e)
PARAMS = pltpu.CompilerParams(vmem_limit_bytes=24 * 2**20)
VMEM = pl.BlockSpec(memory_space=pltpu.VMEM)
NT = (((1,), (1,)), ((), ()))


def call(body, grid, in_specs, out_specs, out_shape, scratch=(), prefetch=0, flops=0, nbytes=0):
    return pl.pallas_call(
        body,
        out_shape=out_shape,
        grid_spec=pltpu.PrefetchScalarGridSpec(
            num_scalar_prefetch=prefetch,
            grid=grid,
            in_specs=in_specs,
            out_specs=out_specs,
            scratch_shapes=list(scratch),
        ),
        compiler_params=PARAMS,
        cost_estimate=pl.CostEstimate(flops=flops, bytes_accessed=nbytes, transcendentals=0),
    )


def far(x):
    return pltpu.with_memory_space_constraint(x, pltpu.HBM)


def sigmoid(x):
    return 0.5 * jnp.tanh(0.5 * x) + 0.5


def dot(a, b, dims=None):
    if dims is None:
        return jnp.dot(a, b, preferred_element_type=jnp.float32)
    return lax.dot_general(a, b, dims, preferred_element_type=jnp.float32)


def steps_of(heads, most=5):
    return next(n for n in range(min(heads, most), 0, -1) if heads % n == 0)


def grad_body(peers, group, chunk, z_ref, k_ref, v_ref, r_ref, w_ref, *refs):
    outs, total = refs[:peers], refs[peers]
    size = w_ref.shape[2]
    rows = k_ref.shape[0]
    own = outs[0].shape[2]
    first = pl.program_id(0) * group
    tasks = [(g, c) for g in range(group) for c in range(0, rows, chunk)]
    turned = {}

    def products(g, c):
        if g not in turned:
            flipped = [jnp.transpose(w_ref[g, m]) for m in range(3)]
            turned[g] = (jnp.concatenate(flipped[:2], axis=0), flipped[2])
        cols, span = slice(g * size, (g + 1) * size), slice(c, c + chunk)
        inner = dot(turned[g][0], k_ref[span, cols], NT)
        return inner, dot(turned[g][1], v_ref[span, cols], NT)

    def finish(g, c, inner, back, sums):
        cols, span = slice(g * size, (g + 1) * size), slice(c, c + chunk)
        rate = r_ref[pl.ds(first + g, 1), span]
        gate, up = inner[:size], inner[size:]
        back = back * rate
        sig = sigmoid(gate)
        silu = gate * sig
        hidden = (silu * (up * rate)).astype(jnp.bfloat16)
        gate_grad = (back * up * (sig + silu * (1.0 - sig))).astype(jnp.bfloat16)
        up_grad = (back * silu).astype(jnp.bfloat16)
        found = [
            dot(jnp.concatenate([gate_grad, up_grad], axis=0), k_ref[span, cols]),
            dot(hidden, v_ref[span, cols]),
        ]
        sums = found if sums is None else [a + b for a, b in zip(sums, found)]
        if c + chunk < rows:
            return sums
        total[g % 2, 0] = jnp.transpose(sums[0][:size])
        total[g % 2, 1] = jnp.transpose(sums[0][size:])
        total[g % 2, 2] = jnp.transpose(sums[1])
        for m in range(peers):
            row = pl.multiple_of((z_ref[0] ^ m) * own, own)
            outs[m][g] = total[g % 2, :, pl.ds(row, own), :].astype(outs[m].dtype)
        return None

    sums = None
    ready = products(*tasks[0])
    for i, task in enumerate(tasks):
        following = products(*tasks[i + 1]) if i + 1 < len(tasks) else None
        sums = finish(*task, *ready, sums)
        ready = following


def partial_grads(z, keys, values, rates, weights, peers, kinds):
    rows = keys.shape[0]
    heads, _, size, _ = weights.shape
    own = size // peers
    group = steps_of(heads)
    column = pl.BlockSpec((rows, group * size), lambda h, z: (0, h))
    return call(
        functools.partial(grad_body, peers, group, min(rows, 256)),
        (heads // group,),
        [
            column,
            column,
            pl.BlockSpec((heads, rows), lambda h, z: (0, 0)),
            pl.BlockSpec((group, 3, size, size), lambda h, z: (h, 0, 0, 0)),
        ],
        [pl.BlockSpec((group, 3, own, size), lambda h, z: (h, 0, 0, 0))] * peers,
        [jax.ShapeDtypeStruct((heads, 3, own, size), kind) for kind in kinds],
        [pltpu.VMEM((2, 3, size, size), jnp.float32)],
        1,
        12 * rows * heads * size * size,
        4 * rows * heads * size,
    )(z, far(keys), far(values), far(rates), far(weights))


def update_body(count, z_ref, w_ref, m_ref, *refs):
    terms, w_out, m_out = refs[:count], refs[count], refs[count + 1]
    for g in range(w_ref.shape[0]):
        new = momentum_keep * m_ref[g]
        for term in terms:
            new = new + term[g].astype(jnp.float32)
        before = w_ref[g].astype(jnp.float32)
        moved = before + new
        ratio = jnp.sqrt(
            (jnp.mean(before * before, axis=-1, keepdims=True) + epsilon)
            / (jnp.mean(moved * moved, axis=-1, keepdims=True) + epsilon)
        )
        m_out[g] = new
        w_out[g] = (moved * ratio).astype(w_out.dtype)


def updated(z, weights, momentum, terms):
    shape = momentum.shape
    whole = pl.BlockSpec(shape, lambda i, z: (0, 0, 0, 0))
    count = momentum.size
    return call(
        functools.partial(update_body, len(terms)),
        (1,),
        [pl.BlockSpec(shape, lambda i, z: (0, 0, z[0], 0)), whole] + [VMEM] * len(terms),
        [VMEM, whole],
        [jax.ShapeDtypeStruct(shape, jnp.bfloat16), jax.ShapeDtypeStruct(shape, jnp.float32)],
        (),
        1,
        20 * count,
        16 * count,
    )(z, weights, momentum, *terms)


def attend(tasks, s_ref):
    def scores(i):
        query, segments, _ = tasks[i]
        query = query()
        top = None
        for j, (key, _, mask) in enumerate(segments):
            score = dot(key(), query, NT)
            if mask is not None:
                score = jnp.where(mask, score, MASKED)
            s_ref[i % 2, j * TILE : (j + 1) * TILE, :] = score
            most = jnp.max(score.reshape(TILE // 8, 8, TILE), axis=0)
            top = most if top is None else jnp.maximum(top, most)
        return jnp.max(top, axis=0, keepdims=True)

    def weigh(i, top):
        _, segments, emit = tasks[i]
        factor = segments[0][0]().shape[1] ** (-0.5)
        out = total = None
        for j, (_, value, _) in enumerate(segments):
            score = s_ref[i % 2, j * TILE : (j + 1) * TILE, :]
            weight = jnp.exp2((score - top) * (factor * LOG2E))
            part = jnp.sum(weight.reshape(TILE // 8, 8, TILE), axis=0)
            product = dot(value(), weight.astype(jnp.bfloat16))
            total = part if total is None else total + part
            out = product if out is None else out + product
        total = jnp.sum(total, axis=0, keepdims=True)
        emit(out * (1.0 / total), top * factor + jnp.log(total))

    top = scores(0)
    for i in range(len(tasks)):
        following = scores(i + 1) if i + 1 < len(tasks) else None
        weigh(i, top)
        top = following


def masks():
    row = lax.broadcasted_iota(jnp.int32, (TILE, TILE), 0)
    col = lax.broadcasted_iota(jnp.int32, (TILE, TILE), 1)
    return row <= col, row > col


def spans(ref, t, cols):
    return lambda: ref[t * TILE : (t + 1) * TILE, cols]


def turned(memo, ref, t, cols, key):
    def load():
        if (key, t) not in memo:
            memo[key, t] = jnp.transpose(ref[t * TILE : (t + 1) * TILE, cols])
        return memo[key, t]

    return load


def put(o_ref, t, cols):
    def emit(out, level):
        o_ref[t * TILE : (t + 1) * TILE, cols] = jnp.transpose(out).astype(o_ref.dtype)

    return emit


SCORES = (WIN // TILE + 1) * TILE


def later_body(group, q_ref, k_ref, v_ref, *refs):
    o_ref, s_ref = refs[-2:]
    size = q_ref.shape[1] // group
    causal, late = masks()
    depth = WIN // TILE
    tasks = []
    for g in range(group):
        cols = slice(g * size, (g + 1) * size)
        memo = {}
        for t in range(depth, q_ref.shape[0] // TILE):
            found = [
                (
                    spans(k_ref, j, cols),
                    turned(memo, v_ref, j, cols, 0),
                    causal if j == t else late if j == t - depth else None,
                )
                for j in range(t - depth, t + 1)
            ]
            tasks.append((spans(q_ref, t, cols), found, put(o_ref, t - depth, cols)))
    attend(tasks, s_ref)


def later_blocks(queries, keys, values, size, step, group, partly):
    rows, width = queries.shape
    column = pl.BlockSpec((rows, group * size), lambda h: (0, step))
    more = [] if partly is None else [partly]
    return pl.pallas_call(
        functools.partial(later_body, group),
        name="later",
        out_shape=jax.ShapeDtypeStruct((rows - WIN, width), jnp.bfloat16),
        grid_spec=pltpu.PrefetchScalarGridSpec(
            num_scalar_prefetch=0,
            grid=(1,),
            in_specs=[column] * 3 + [pl.BlockSpec(memory_space=pl.ANY)] * len(more),
            out_specs=pl.BlockSpec((rows - WIN, group * size), lambda h: (0, step)),
            scratch_shapes=[pltpu.VMEM((2, SCORES, TILE), jnp.float32)],
        ),
        compiler_params=PARAMS,
        input_output_aliases={3: 0} if more else {},
        cost_estimate=pl.CostEstimate(
            flops=6 * (rows - WIN) * WIN * size * group,
            bytes_accessed=8 * rows * size * group,
            transcendentals=0,
        ),
    )(far(queries), far(keys), far(values), *more)


def carried_body(group, z_ref, q_ref, k_ref, v_ref, p_ref, o_ref, s_ref):
    size = q_ref.shape[1] // group
    causal, late = masks()
    depth = WIN // TILE
    there = jnp.broadcast_to(z_ref[0] > 0, causal.shape)
    tasks = []
    for g in range(group):
        cols = slice(g * size, (g + 1) * size)
        memo = {}
        for t in range(depth):
            found = [
                (spans(p_ref.at[0], j, cols), turned(memo, p_ref.at[1], j, cols, 1), late & there if j == t else there)
                for j in range(t, depth)
            ]
            found += [
                (spans(k_ref, j, cols), turned(memo, v_ref, j, cols, 0), causal if j == t else None)
                for j in range(t + 1)
            ]
            tasks.append((spans(q_ref, t, cols), found, put(o_ref, t, cols)))
    attend(tasks, s_ref)


def carried_block(z, queries, keys, values, carried, size):
    heads = carried.shape[2] // size
    group = heads
    width = queries.shape[1]
    column = pl.BlockSpec((WIN, group * size), lambda h, z: (0, h))
    return call(
        functools.partial(carried_body, group),
        (heads // group,),
        [column] * 3 + [VMEM],
        column,
        jax.ShapeDtypeStruct((WIN, width), jnp.bfloat16),
        [pltpu.VMEM((2, SCORES, TILE), jnp.float32)],
        1,
        6 * WIN * WIN * size * heads,
        10 * WIN * size * heads,
    )(z, queries, keys, values, carried)


EXTRA = 8
KEPT = 3
EARLY = 5


def put_partial(o_ref, g, t, size):
    def emit(out, level):
        span = slice(t * TILE, (t + 1) * TILE)
        o_ref[g, :size, span] = out.astype(o_ref.dtype)
        rest, parts = level, []
        for _ in range(3):
            term = rest.astype(jnp.bfloat16).astype(jnp.float32)
            parts.append(term)
            rest = rest - term
        parts.append(jnp.zeros((EXTRA - 3, TILE), jnp.float32))
        o_ref[g, size:, span] = jnp.concatenate(parts, axis=0).astype(o_ref.dtype)

    return emit


def next_part_body(group, q_ref, k_ref, v_ref, o_ref, s_ref):
    size = q_ref.shape[1] // group
    _, late = masks()
    depth = WIN // TILE
    tasks = []
    for g in range(group):
        cols = slice(g * size, (g + 1) * size)
        memo = {}
        for t in range(depth):
            found = [
                (spans(k_ref, j, cols), turned(memo, v_ref, j, cols, 0), late if j == t else None)
                for j in range(t, depth)
            ]
            tasks.append((spans(q_ref, t, cols), found, put_partial(o_ref, g, t, size)))
    attend(tasks, s_ref)


def next_part(asked, keys, values, first, size):
    heads = asked.shape[1] // size
    block = keys.shape[0] // WIN - 1
    group = math.gcd(heads, first)
    column = pl.BlockSpec((WIN, group * size), lambda h: (block, h + first // group))
    return call(
        functools.partial(next_part_body, group),
        (heads // group,),
        [pl.BlockSpec((WIN, group * size), lambda h: (0, h)), column, column],
        pl.BlockSpec((group, size + EXTRA, WIN), lambda h: (h, 0, 0)),
        jax.ShapeDtypeStruct((heads, size + EXTRA, WIN), jnp.bfloat16),
        [pltpu.VMEM((2, WIN, TILE), jnp.float32)],
        0,
        4 * WIN * WIN * size * heads,
        8 * WIN * size * heads,
    )(asked, keys, values)


def joined_body(group, z_ref, q_ref, k_ref, v_ref, p_ref, _, o_ref, s_ref):
    size = q_ref.shape[1] // group
    causal, _ = masks()
    depth = WIN // TILE
    step = pl.program_id(0) * group

    def join(g, t, cols):
        def emit(out, level):
            span = slice(t * TILE, (t + 1) * TILE)
            terms = p_ref[step + g, size:, span].astype(jnp.float32)
            other = terms[0:1] + (terms[1:2] + terms[2:3])
            share = jnp.where(z_ref[0] > 0, jax.nn.sigmoid(other - level), 0.0)
            out = out + share * (p_ref[step + g, :size, span].astype(jnp.float32) - out)
            o_ref[span, cols] = jnp.transpose(out).astype(o_ref.dtype)

        return emit

    tasks = []
    for g in range(group):
        cols = slice(g * size, (g + 1) * size)
        memo = {}
        for t in range(depth):
            found = [
                (spans(k_ref, j, cols), turned(memo, v_ref, j, cols, 0), causal if j == t else None)
                for j in range(t + 1)
            ]
            tasks.append((spans(q_ref, t, cols), found, join(g, t, cols)))
    attend(tasks, s_ref)


def joined_block(z, queries, keys, values, given, partly, first, size):
    heads = given.shape[0]
    group = math.gcd(heads, first)
    column = pl.BlockSpec((WIN, group * size), lambda h, z: (0, h + first // group))
    return pl.pallas_call(
        functools.partial(joined_body, group),
        name="joined",
        out_shape=jax.ShapeDtypeStruct(partly.shape, partly.dtype),
        grid_spec=pltpu.PrefetchScalarGridSpec(
            num_scalar_prefetch=1,
            grid=(heads // group,),
            in_specs=[
                column,
                column,
                column,
                VMEM,
                pl.BlockSpec(memory_space=pl.ANY),
            ],
            out_specs=column,
            scratch_shapes=[pltpu.VMEM((2, WIN, TILE), jnp.float32)],
        ),
        compiler_params=PARAMS,
        input_output_aliases={5: 0},
        cost_estimate=pl.CostEstimate(
            flops=4 * WIN * WIN * size * heads, bytes_accessed=10 * WIN * size * heads, transcendentals=0
        ),
    )(z, queries, keys, values, given, partly)


def final_body(peers, group, start, z_ref, q_ref, first_ref, later_ref, *refs):
    blocks, o_ref, whole = refs[:peers], refs[-2], refs[-1]
    size = q_ref.shape[1] // group
    own = blocks[0].shape[2]
    for m in range(peers):
        row = pl.multiple_of((z_ref[0] ^ m) * own, own)
        base = start if m + 1 < peers else 0
        whole[:, :, pl.ds(row, own), :] = blocks[m][base : base + group].astype(whole.dtype)
    tasks = [(g, c) for g in range(group) for c in range(0, q_ref.shape[0], WIN)]

    def products(g, c):
        query = q_ref[c : c + WIN, g * size : (g + 1) * size]
        both = jnp.concatenate([whole[g, 0], whole[g, 1]], axis=1).astype(jnp.bfloat16)
        return dot(query, both)

    def finish(g, c, inner):
        cols = slice(g * size, (g + 1) * size)
        gate, up = inner[:, :size], inner[:, size:]
        hidden = (gate * sigmoid(gate) * up).astype(jnp.bfloat16)
        fast = dot(hidden, whole[g, 2].astype(jnp.bfloat16), NT)
        kept = first_ref[:, cols] if c == 0 else later_ref[c - WIN : c, cols]
        o_ref[c : c + WIN, cols] = (fast + kept.astype(jnp.float32)).astype(o_ref.dtype)

    ready = products(*tasks[0])
    for i, task in enumerate(tasks):
        following = products(*tasks[i + 1]) if i + 1 < len(tasks) else None
        finish(*task, ready)
        ready = following


def final(z, queries, first, later, blocks, size, step, group, partly):
    rows, width = queries.shape
    peers, own = len(blocks), blocks[0].shape[2]
    kind = jnp.bfloat16 if own % 16 == 0 else jnp.float32
    more = [] if partly is None else [partly]
    return pl.pallas_call(
        functools.partial(final_body, peers, group, step * group),
        name="final",
        out_shape=jax.ShapeDtypeStruct((rows, width), jnp.bfloat16),
        grid_spec=pltpu.PrefetchScalarGridSpec(
            num_scalar_prefetch=1,
            grid=(1,),
            in_specs=[
                pl.BlockSpec((rows, group * size), lambda h, z: (0, step)),
                pl.BlockSpec((WIN, group * size), lambda h, z: (0, step)),
                pl.BlockSpec((rows - WIN, group * size), lambda h, z: (0, step)),
            ]
            + [VMEM] * peers
            + [pl.BlockSpec(memory_space=pl.ANY)] * len(more),
            out_specs=pl.BlockSpec((rows, group * size), lambda h, z: (0, step)),
            scratch_shapes=[pltpu.VMEM((group, 3, size, size), kind)],
        ),
        compiler_params=PARAMS,
        input_output_aliases={4 + peers: 0} if more else {},
        cost_estimate=pl.CostEstimate(
            flops=6 * rows * group * size * size,
            bytes_accessed=6 * rows * group * size,
            transcendentals=0,
        ),
    )(z, queries, first, later, *blocks, *more)


def pack_body(first, q_ref, k_ref, v_ref, ask_ref, carry_ref, sems):
    cut = carry_ref.shape[2]
    tail = pl.ds(q_ref.shape[0] - WIN, WIN)
    copies = [
        (k_ref.at[tail, pl.ds(0, cut)], carry_ref.at[0]),
        (v_ref.at[tail, pl.ds(0, cut)], carry_ref.at[1]),
        (q_ref.at[pl.ds(0, WIN), pl.ds(first, ask_ref.shape[1])], ask_ref),
    ]
    copies = [pltpu.make_async_copy(*c, sems.at[i]) for i, c in enumerate(copies)]
    for copy in copies:
        copy.start()
    for copy in copies:
        copy.wait()


def packed(queries, keys, values, cut, asked):
    here = pl.BlockSpec(memory_space=pltpu.HBM)
    shapes = [(WIN, asked[1]), (2, WIN, cut)]
    return call(
        functools.partial(pack_body, asked[0]),
        (),
        [here] * 3,
        [VMEM] * 2,
        [jax.ShapeDtypeStruct(shape, queries.dtype) for shape in shapes],
        [pltpu.SemaphoreType.DMA((3,))],
        0,
        0,
        4 * WIN * (2 * cut + asked[1]),
    )(far(queries), far(keys), far(values))


def moved_by(value, by):
    peers = lax.axis_size("seq")
    pairs = [(i, i + by) for i in range(peers) if 0 <= i + by < peers]
    return lax.ppermute(value, "seq", pairs)


def swapped(value, mask):
    return lax.ppermute(value, "seq", [(i, i ^ mask) for i in range(lax.axis_size("seq"))])


def kept_of(heads):
    return max(1, heads * KEPT // 10)


def shards(queries, keys, values, rates, fast_weights, momentum):
    heads = rates.shape[0]
    size = fast_weights.shape[0]
    peers = lax.axis_size("seq")
    kept = kept_of(heads)
    z = lax.axis_index("seq").astype(jnp.int32).reshape(1)
    early = max(1, heads * EARLY // 10)
    groups = [(kept, early), (kept + early, heads - kept - early)]

    asked, carried = packed(queries, keys, values, kept * size, (kept * size, early * size))
    asked = [moved_by(asked, -1)]
    asked.append(moved_by(queries[:WIN, (kept + early) * size :], -1))
    carried = moved_by(carried, 1)

    weights = jnp.transpose(fast_weights, (1, 2, 0, 3))
    own_momentum = jnp.transpose(momentum, (1, 2, 0, 3))
    kinds = [jnp.bfloat16 if m % 2 else jnp.float32 for m in range(peers)]
    sums = [[block] for block in partial_grads(z, keys, values, rates, weights, peers, kinds)]

    step = 1
    while step < peers:
        for m in reversed(range(peers)):
            if m % (2 * step) == step:
                terms = sums[m]
                block = functools.reduce(jnp.add, [t.astype(jnp.float32) for t in terms])
                sums[m - step].append(swapped(block.astype(jnp.bfloat16), step))
        step *= 2

    group = steps_of(heads)
    later = None
    for part in range(heads // group):
        later = later_blocks(queries, keys, values, size, part, group, later)
    given = []
    for i, (place, _) in enumerate(groups):
        part = next_part(asked[i], keys, values, place, size)
        given.append(moved_by(part, 1))
    first = carried_block(z, queries, keys, values, carried, size)
    for i, (place, _) in enumerate(groups):
        first = joined_block(z, queries, keys, values, given[i], first, place, size)

    new_rows, new_momentum = updated(z, weights, own_momentum, sums[0])
    blocks = {0: new_rows}
    step = peers // 2
    while step:
        for m in sorted(blocks):
            if m + step < peers - 1:
                blocks[m + step] = swapped(blocks[m], step)
        step //= 2

    mixed = None
    for part in range(heads // group):
        last = swapped(blocks[peers - 2][part * group : (part + 1) * group], 1)
        parts = [blocks[m] for m in range(peers - 1)] + [last]
        mixed = final(z, queries, first, later, parts, size, part, group, mixed)
    return (mixed, jnp.transpose(new_rows, (2, 0, 1, 3)), jnp.transpose(new_momentum, (2, 0, 1, 3)))


def solution(mesh):
    return jax.shard_map(
        shards,
        mesh=mesh,
        in_specs=(
            P(("groups", "seq"), ("head", "rep")),
            P(("groups", "seq"), ("head", "rep")),
            P(("groups", "seq"), ("head", "rep")),
            P(("head", "rep"), ("groups", "seq")),
            P(None, ("head", "rep"), None, None),
            P("seq", ("head", "rep"), None, None),
        ),
        out_specs=(
            P(("groups", "seq"), ("head", "rep")),
            P(("groups", "seq"), ("head", "rep"), None, None),
            P(("groups", "seq"), ("head", "rep"), None, None),
        ),
        check_vma=False,
    )
```

```python
import functools
import math

import jax
import jax.numpy as jnp
from jax import lax
from jax.experimental import pallas as pl
from jax.experimental.pallas import tpu as pltpu
from jax.sharding import PartitionSpec as P


WIN = 512
TILE = 256

momentum_keep = 0.9
epsilon = 1e-06
MASKED = -1e30
LOG2E = math.log2(math.e)
PARAMS = pltpu.CompilerParams(vmem_limit_bytes=24 * 2**20)
VMEM = pl.BlockSpec(memory_space=pltpu.VMEM)
NT = (((1,), (1,)), ((), ()))


def call(body, grid, in_specs, out_specs, out_shape, scratch=(), prefetch=0, flops=0, nbytes=0):
    return pl.pallas_call(
        body,
        out_shape=out_shape,
        grid_spec=pltpu.PrefetchScalarGridSpec(
            num_scalar_prefetch=prefetch,
            grid=grid,
            in_specs=in_specs,
            out_specs=out_specs,
            scratch_shapes=list(scratch),
        ),
        compiler_params=PARAMS,
        cost_estimate=pl.CostEstimate(flops=flops, bytes_accessed=nbytes, transcendentals=0),
    )


def far(x):
    return pltpu.with_memory_space_constraint(x, pltpu.HBM)


def sigmoid(x):
    return 0.5 * jnp.tanh(0.5 * x) + 0.5


def dot(a, b, dims=None):
    if dims is None:
        return jnp.dot(a, b, preferred_element_type=jnp.float32)
    return lax.dot_general(a, b, dims, preferred_element_type=jnp.float32)


def steps_of(heads, most=5):
    return next(n for n in range(min(heads, most), 0, -1) if heads % n == 0)


def grad_body(peers, group, chunk, z_ref, k_ref, v_ref, r_ref, w_ref, *refs):
    outs, total = refs[:peers], refs[peers]
    size = w_ref.shape[2]
    rows = k_ref.shape[0]
    own = outs[0].shape[2]
    first = pl.program_id(0) * group
    tasks = [(g, c) for g in range(group) for c in range(0, rows, chunk)]
    turned = {}

    def products(g, c):
        if g not in turned:
            flipped = [jnp.transpose(w_ref[g, m]) for m in range(3)]
            turned[g] = (jnp.concatenate(flipped[:2], axis=0), flipped[2])
        cols, span = slice(g * size, (g + 1) * size), slice(c, c + chunk)
        inner = dot(turned[g][0], k_ref[span, cols], NT)
        return inner, dot(turned[g][1], v_ref[span, cols], NT)

    def finish(g, c, inner, back, sums):
        cols, span = slice(g * size, (g + 1) * size), slice(c, c + chunk)
        rate = r_ref[pl.ds(first + g, 1), span]
        gate, up = inner[:size], inner[size:]
        back = back * rate
        sig = sigmoid(gate)
        silu = gate * sig
        hidden = (silu * (up * rate)).astype(jnp.bfloat16)
        gate_grad = (back * up * (sig + silu * (1.0 - sig))).astype(jnp.bfloat16)
        up_grad = (back * silu).astype(jnp.bfloat16)
        found = [
            dot(jnp.concatenate([gate_grad, up_grad], axis=0), k_ref[span, cols]),
            dot(hidden, v_ref[span, cols]),
        ]
        sums = found if sums is None else [a + b for a, b in zip(sums, found)]
        if c + chunk < rows:
            return sums
        total[g % 2, 0] = jnp.transpose(sums[0][:size])
        total[g % 2, 1] = jnp.transpose(sums[0][size:])
        total[g % 2, 2] = jnp.transpose(sums[1])
        for m in range(peers):
            row = pl.multiple_of((z_ref[0] ^ m) * own, own)
            outs[m][g] = total[g % 2, :, pl.ds(row, own), :].astype(outs[m].dtype)
        return None

    sums = None
    ready = products(*tasks[0])
    for i, task in enumerate(tasks):
        following = products(*tasks[i + 1]) if i + 1 < len(tasks) else None
        sums = finish(*task, *ready, sums)
        ready = following


def partial_grads(z, keys, values, rates, weights, peers, kinds):
    rows = keys.shape[0]
    heads, _, size, _ = weights.shape
    own = size // peers
    group = steps_of(heads)
    column = pl.BlockSpec((rows, group * size), lambda h, z: (0, h))
    return call(
        functools.partial(grad_body, peers, group, min(rows, 256)),
        (heads // group,),
        [
            column,
            column,
            pl.BlockSpec((heads, rows), lambda h, z: (0, 0)),
            pl.BlockSpec((group, 3, size, size), lambda h, z: (h, 0, 0, 0)),
        ],
        [pl.BlockSpec((group, 3, own, size), lambda h, z: (h, 0, 0, 0))] * peers,
        [jax.ShapeDtypeStruct((heads, 3, own, size), kind) for kind in kinds],
        [pltpu.VMEM((2, 3, size, size), jnp.float32)],
        1,
        12 * rows * heads * size * size,
        4 * rows * heads * size,
    )(z, far(keys), far(values), far(rates), far(weights))


def update_body(count, z_ref, w_ref, m_ref, *refs):
    terms, w_out, m_out = refs[:count], refs[count], refs[count + 1]
    for g in range(w_ref.shape[0]):
        new = momentum_keep * m_ref[g]
        for term in terms:
            new = new + term[g].astype(jnp.float32)
        before = w_ref[g].astype(jnp.float32)
        moved = before + new
        ratio = jnp.sqrt(
            (jnp.mean(before * before, axis=-1, keepdims=True) + epsilon)
            / (jnp.mean(moved * moved, axis=-1, keepdims=True) + epsilon)
        )
        m_out[g] = new
        w_out[g] = (moved * ratio).astype(w_out.dtype)


def updated(z, weights, momentum, terms):
    shape = momentum.shape
    whole = pl.BlockSpec(shape, lambda i, z: (0, 0, 0, 0))
    count = momentum.size
    return call(
        functools.partial(update_body, len(terms)),
        (1,),
        [pl.BlockSpec(shape, lambda i, z: (0, 0, z[0], 0)), whole] + [VMEM] * len(terms),
        [VMEM, whole],
        [jax.ShapeDtypeStruct(shape, jnp.bfloat16), jax.ShapeDtypeStruct(shape, jnp.float32)],
        (),
        1,
        20 * count,
        16 * count,
    )(z, weights, momentum, *terms)


def attend(tasks, s_ref):
    def scores(i):
        query, segments, _ = tasks[i]
        query = query()
        top = None
        for j, (key, _, mask) in enumerate(segments):
            score = dot(key(), query, NT)
            if mask is not None:
                score = jnp.where(mask, score, MASKED)
            s_ref[i % 2, j * TILE : (j + 1) * TILE, :] = score
            most = jnp.max(score.reshape(TILE // 8, 8, TILE), axis=0)
            top = most if top is None else jnp.maximum(top, most)
        return jnp.max(top, axis=0, keepdims=True)

    def weigh(i, top):
        _, segments, emit = tasks[i]
        factor = segments[0][0]().shape[1] ** (-0.5)
        out = total = None
        for j, (_, value, _) in enumerate(segments):
            score = s_ref[i % 2, j * TILE : (j + 1) * TILE, :]
            weight = jnp.exp2((score - top) * (factor * LOG2E))
            part = jnp.sum(weight.reshape(TILE // 8, 8, TILE), axis=0)
            product = dot(value(), weight.astype(jnp.bfloat16))
            total = part if total is None else total + part
            out = product if out is None else out + product
        total = jnp.sum(total, axis=0, keepdims=True)
        emit(out * (1.0 / total), top * factor + jnp.log(total))

    top = scores(0)
    for i in range(len(tasks)):
        following = scores(i + 1) if i + 1 < len(tasks) else None
        weigh(i, top)
        top = following


def masks():
    row = lax.broadcasted_iota(jnp.int32, (TILE, TILE), 0)
    col = lax.broadcasted_iota(jnp.int32, (TILE, TILE), 1)
    return row <= col, row > col


def spans(ref, t, cols):
    return lambda: ref[t * TILE : (t + 1) * TILE, cols]


def turned(memo, ref, t, cols, key):
    def load():
        if (key, t) not in memo:
            memo[key, t] = jnp.transpose(ref[t * TILE : (t + 1) * TILE, cols])
        return memo[key, t]

    return load


def put(o_ref, t, cols):
    def emit(out, level):
        o_ref[t * TILE : (t + 1) * TILE, cols] = jnp.transpose(out).astype(o_ref.dtype)

    return emit


SCORES = (WIN // TILE + 1) * TILE


def later_body(group, q_ref, k_ref, v_ref, *refs):
    o_ref, s_ref = refs[-2:]
    size = q_ref.shape[1] // group
    causal, late = masks()
    depth = WIN // TILE
    tasks = []
    for g in range(group):
        cols = slice(g * size, (g + 1) * size)
        memo = {}
        for t in range(depth, q_ref.shape[0] // TILE):
            found = [
                (
                    spans(k_ref, j, cols),
                    turned(memo, v_ref, j, cols, 0),
                    causal if j == t else late if j == t - depth else None,
                )
                for j in range(t - depth, t + 1)
            ]
            tasks.append((spans(q_ref, t, cols), found, put(o_ref, t - depth, cols)))
    attend(tasks, s_ref)


def later_blocks(queries, keys, values, size, step, group, partly):
    rows, width = queries.shape
    column = pl.BlockSpec((rows, group * size), lambda h: (0, step))
    more = [] if partly is None else [partly]
    return pl.pallas_call(
        functools.partial(later_body, group),
        name="later",
        out_shape=jax.ShapeDtypeStruct((rows - WIN, width), jnp.bfloat16),
        grid_spec=pltpu.PrefetchScalarGridSpec(
            num_scalar_prefetch=0,
            grid=(1,),
            in_specs=[column] * 3 + [pl.BlockSpec(memory_space=pl.ANY)] * len(more),
            out_specs=pl.BlockSpec((rows - WIN, group * size), lambda h: (0, step)),
            scratch_shapes=[pltpu.VMEM((2, SCORES, TILE), jnp.float32)],
        ),
        compiler_params=PARAMS,
        input_output_aliases={3: 0} if more else {},
        cost_estimate=pl.CostEstimate(
            flops=6 * (rows - WIN) * WIN * size * group,
            bytes_accessed=8 * rows * size * group,
            transcendentals=0,
        ),
    )(*[x if more else far(x) for x in (queries, keys, values)], *more)


def carried_body(group, z_ref, q_ref, k_ref, v_ref, p_ref, o_ref, s_ref):
    size = q_ref.shape[1] // group
    causal, late = masks()
    depth = WIN // TILE
    there = jnp.broadcast_to(z_ref[0] > 0, causal.shape)
    tasks = []
    for g in range(group):
        cols = slice(g * size, (g + 1) * size)
        memo = {}
        for t in range(depth):
            found = [
                (spans(p_ref.at[0], j, cols), turned(memo, p_ref.at[1], j, cols, 1), late & there if j == t else there)
                for j in range(t, depth)
            ]
            found += [
                (spans(k_ref, j, cols), turned(memo, v_ref, j, cols, 0), causal if j == t else None)
                for j in range(t + 1)
            ]
            tasks.append((spans(q_ref, t, cols), found, put(o_ref, t, cols)))
    attend(tasks, s_ref)


def carried_block(z, queries, keys, values, carried, size):
    heads = carried.shape[2] // size
    group = heads
    width = queries.shape[1]
    column = pl.BlockSpec((WIN, group * size), lambda h, z: (0, h))
    return call(
        functools.partial(carried_body, group),
        (heads // group,),
        [column] * 3 + [VMEM],
        column,
        jax.ShapeDtypeStruct((WIN, width), jnp.bfloat16),
        [pltpu.VMEM((2, SCORES, TILE), jnp.float32)],
        1,
        6 * WIN * WIN * size * heads,
        10 * WIN * size * heads,
    )(z, queries, keys, values, carried)


EXTRA = 8
KEPT = 3
EARLY = 5


def put_partial(o_ref, g, t, size):
    def emit(out, level):
        span = slice(t * TILE, (t + 1) * TILE)
        o_ref[g, :size, span] = out.astype(o_ref.dtype)
        rest, parts = level, []
        for _ in range(3):
            term = rest.astype(jnp.bfloat16).astype(jnp.float32)
            parts.append(term)
            rest = rest - term
        parts.append(jnp.zeros((EXTRA - 3, TILE), jnp.float32))
        o_ref[g, size:, span] = jnp.concatenate(parts, axis=0).astype(o_ref.dtype)

    return emit


def next_part_body(group, skip, q_ref, k_ref, v_ref, o_ref, s_ref):
    size = k_ref.shape[1] // group
    start = skip + pl.program_id(0) * group if q_ref.shape[1] > group * size else 0
    _, late = masks()
    depth = WIN // TILE
    tasks = []
    for g in range(group):
        cols = slice(g * size, (g + 1) * size)
        memo = {}
        for t in range(depth):
            found = [
                (spans(k_ref, j, cols), turned(memo, v_ref, j, cols, 0), late if j == t else None)
                for j in range(t, depth)
            ]
            lanes = pl.ds(pl.multiple_of((start + g) * size, size), size)
            tasks.append((spans(q_ref, t, lanes), found, put_partial(o_ref, g, t, size)))
    attend(tasks, s_ref)


def next_part(asked, keys, values, skip, first, heads, size):
    block = keys.shape[0] // WIN - 1
    group = math.gcd(heads, first)
    column = pl.BlockSpec((WIN, group * size), lambda h: (block, h + first // group))
    return call(
        functools.partial(next_part_body, group, skip),
        (heads // group,),
        [VMEM, column, column],
        pl.BlockSpec((group, size + EXTRA, WIN), lambda h: (h, 0, 0)),
        jax.ShapeDtypeStruct((heads, size + EXTRA, WIN), jnp.bfloat16),
        [pltpu.VMEM((2, WIN, TILE), jnp.float32)],
        0,
        4 * WIN * WIN * size * heads,
        8 * WIN * size * heads,
    )(asked, keys, values)


def joined_body(group, add, z_ref, q_ref, k_ref, v_ref, p_ref, base_ref, o_ref, s_ref):
    size = q_ref.shape[1] // group
    causal, _ = masks()
    depth = WIN // TILE
    step = pl.program_id(0) * group

    def join(g, t, cols):
        def emit(out, level):
            span = slice(t * TILE, (t + 1) * TILE)
            terms = p_ref[step + g, size:, span].astype(jnp.float32)
            other = terms[0:1] + (terms[1:2] + terms[2:3])
            share = jnp.where(z_ref[0] > 0, jax.nn.sigmoid(other - level), 0.0)
            out = out + share * (p_ref[step + g, :size, span].astype(jnp.float32) - out)
            out = jnp.transpose(out)
            if add:
                out = out + base_ref[span, cols].astype(jnp.float32)
            o_ref[span, cols] = out.astype(o_ref.dtype)

        return emit

    tasks = []
    for g in range(group):
        cols = slice(g * size, (g + 1) * size)
        memo = {}
        for t in range(depth):
            found = [
                (spans(k_ref, j, cols), turned(memo, v_ref, j, cols, 0), causal if j == t else None)
                for j in range(t + 1)
            ]
            tasks.append((spans(q_ref, t, cols), found, join(g, t, cols)))
    attend(tasks, s_ref)


def joined_block(z, queries, keys, values, given, partly, first, size, add):
    heads = given.shape[0]
    group = math.gcd(heads, first)
    column = pl.BlockSpec((WIN, group * size), lambda h, z: (0, h + first // group))
    return pl.pallas_call(
        functools.partial(joined_body, group, add),
        name="joined",
        out_shape=jax.ShapeDtypeStruct(partly.shape, partly.dtype),
        grid_spec=pltpu.PrefetchScalarGridSpec(
            num_scalar_prefetch=1,
            grid=(heads // group,),
            in_specs=[
                column,
                column,
                column,
                VMEM,
                column if add else pl.BlockSpec(memory_space=pl.ANY),
            ],
            out_specs=column,
            scratch_shapes=[pltpu.VMEM((2, WIN, TILE), jnp.float32)],
        ),
        compiler_params=PARAMS,
        input_output_aliases={5: 0},
        cost_estimate=pl.CostEstimate(
            flops=4 * WIN * WIN * size * heads, bytes_accessed=10 * WIN * size * heads, transcendentals=0
        ),
    )(z, queries, keys, values, given, partly)


def final_body(peers, group, start, limit, z_ref, q_ref, first_ref, later_ref, *refs):
    blocks, o_ref, whole = refs[:peers], refs[-2], refs[-1]
    size = q_ref.shape[1] // group
    own = blocks[0].shape[2]
    for m in range(peers):
        row = pl.multiple_of((z_ref[0] ^ m) * own, own)
        base = start if m + 1 < peers else 0
        whole[:, :, pl.ds(row, own), :] = blocks[m][base : base + group].astype(whole.dtype)
    tasks = [(g, c) for g in range(group) for c in range(0, q_ref.shape[0], WIN)]

    def products(g, c):
        query = q_ref[c : c + WIN, g * size : (g + 1) * size]
        both = jnp.concatenate([whole[g, 0], whole[g, 1]], axis=1).astype(jnp.bfloat16)
        return dot(query, both)

    def finish(g, c, inner):
        cols = slice(g * size, (g + 1) * size)
        gate, up = inner[:, :size], inner[:, size:]
        hidden = (gate * sigmoid(gate) * up).astype(jnp.bfloat16)
        fast = dot(hidden, whole[g, 2].astype(jnp.bfloat16), NT)
        if c or start + g < limit:
            kept = later_ref[c - WIN : c, cols] if c else first_ref[:, cols]
            fast = fast + kept.astype(jnp.float32)
        o_ref[c : c + WIN, cols] = fast.astype(o_ref.dtype)

    ready = products(*tasks[0])
    for i, task in enumerate(tasks):
        following = products(*tasks[i + 1]) if i + 1 < len(tasks) else None
        finish(*task, ready)
        ready = following


def final(z, queries, first, later, blocks, size, step, group, limit, partly):
    rows, width = queries.shape
    peers, own = len(blocks), blocks[0].shape[2]
    kind = jnp.bfloat16 if own % 16 == 0 else jnp.float32
    more = [] if partly is None else [partly]
    return pl.pallas_call(
        functools.partial(final_body, peers, group, step * group, limit),
        name="final",
        out_shape=jax.ShapeDtypeStruct((rows, width), jnp.bfloat16),
        grid_spec=pltpu.PrefetchScalarGridSpec(
            num_scalar_prefetch=1,
            grid=(1,),
            in_specs=[
                pl.BlockSpec((rows, group * size), lambda h, z: (0, step)),
                pl.BlockSpec((WIN, group * size), lambda h, z: (0, step)),
                pl.BlockSpec((rows - WIN, group * size), lambda h, z: (0, step)),
            ]
            + [VMEM] * peers
            + [pl.BlockSpec(memory_space=pl.ANY)] * len(more),
            out_specs=pl.BlockSpec((rows, group * size), lambda h, z: (0, step)),
            scratch_shapes=[pltpu.VMEM((group, 3, size, size), kind)],
        ),
        compiler_params=PARAMS,
        input_output_aliases={4 + peers: 0} if more else {},
        cost_estimate=pl.CostEstimate(
            flops=6 * rows * group * size * size,
            bytes_accessed=6 * rows * group * size,
            transcendentals=0,
        ),
    )(z, queries, first, later, *blocks, *more)


def pack_body(first, q_ref, k_ref, v_ref, ask_ref, carry_ref, sems):
    cut = carry_ref.shape[2]
    tail = pl.ds(q_ref.shape[0] - WIN, WIN)
    copies = [
        (k_ref.at[tail, pl.ds(0, cut)], carry_ref.at[0]),
        (v_ref.at[tail, pl.ds(0, cut)], carry_ref.at[1]),
        (q_ref.at[pl.ds(0, WIN), pl.ds(first, ask_ref.shape[1])], ask_ref),
    ]
    copies = [pltpu.make_async_copy(*c, sems.at[i]) for i, c in enumerate(copies)]
    for copy in copies:
        copy.start()
    for copy in copies:
        copy.wait()


def packed(queries, keys, values, cut, asked):
    here = pl.BlockSpec(memory_space=pltpu.HBM)
    shapes = [(WIN, asked[1]), (2, WIN, cut)]
    return call(
        functools.partial(pack_body, asked[0]),
        (),
        [here] * 3,
        [VMEM] * 2,
        [jax.ShapeDtypeStruct(shape, queries.dtype) for shape in shapes],
        [pltpu.SemaphoreType.DMA((3,))],
        0,
        0,
        4 * WIN * (2 * cut + asked[1]),
    )(far(queries), far(keys), far(values))


def moved_by(value, by):
    peers = lax.axis_size("seq")
    pairs = [(i, i + by) for i in range(peers) if 0 <= i + by < peers]
    return lax.ppermute(value, "seq", pairs)


def swapped(value, mask):
    return lax.ppermute(value, "seq", [(i, i ^ mask) for i in range(lax.axis_size("seq"))])


def kept_of(heads):
    return max(1, heads * KEPT // 10)


def shards(queries, keys, values, rates, fast_weights, momentum):
    heads = rates.shape[0]
    size = fast_weights.shape[0]
    peers = lax.axis_size("seq")
    kept = kept_of(heads)
    z = lax.axis_index("seq").astype(jnp.int32).reshape(1)
    early = max(1, heads * EARLY // 10)
    late = kept + early
    lead = (early + 1) // 2
    groups = [(kept, lead, 0, 0), (kept + lead, early - lead, 0, lead), (late, heads - late, 1, 0)]

    asked, carried = packed(queries, keys, values, kept * size, (kept * size, early * size))
    asked = [moved_by(asked, -1)]
    asked.append(moved_by(queries[:WIN, late * size :], -1))
    carried = moved_by(carried, 1)

    weights = jnp.transpose(fast_weights, (1, 2, 0, 3))
    own_momentum = jnp.transpose(momentum, (1, 2, 0, 3))
    kinds = [jnp.bfloat16 if m % 2 else jnp.float32 for m in range(peers)]
    sums = [[block] for block in partial_grads(z, keys, values, rates, weights, peers, kinds)]

    step = 1
    while step < peers:
        for m in reversed(range(peers)):
            if m % (2 * step) == step:
                terms = sums[m]
                block = functools.reduce(jnp.add, [t.astype(jnp.float32) for t in terms])
                sums[m - step].append(swapped(block.astype(jnp.bfloat16), step))
        step *= 2

    group = steps_of(heads)
    later = None
    for part in range(heads // group):
        later = later_blocks(queries, keys, values, size, part, group, later)
    given = []
    for place, count, source, skip in groups:
        part = next_part(asked[source], keys, values, skip, place, count, size)
        given.append(moved_by(part, 1))
    first = carried_block(z, queries, keys, values, carried, size)
    for i, (place, _, _, _) in enumerate(groups[:-1]):
        first = joined_block(z, queries, keys, values, given[i], first, place, size, False)

    new_rows, new_momentum = updated(z, weights, own_momentum, sums[0])
    blocks = {0: new_rows}
    step = peers // 2
    while step:
        for m in sorted(blocks):
            if m + step < peers - 1:
                blocks[m + step] = swapped(blocks[m], step)
        step //= 2

    mixed = None
    for part in range(heads // group):
        last = swapped(blocks[peers - 2][part * group : (part + 1) * group], 1)
        parts = [blocks[m] for m in range(peers - 1)] + [last]
        mixed = final(z, queries, first, later, parts, size, part, group, groups[-1][0], mixed)
    place = groups[-1][0]
    mixed = joined_block(z, queries, keys, values, given[-1], mixed, place, size, True)
    return (mixed, jnp.transpose(new_rows, (2, 0, 1, 3)), jnp.transpose(new_momentum, (2, 0, 1, 3)))


def solution(mesh):
    return jax.shard_map(
        shards,
        mesh=mesh,
        in_specs=(
            P(("groups", "seq"), ("head", "rep")),
            P(("groups", "seq"), ("head", "rep")),
            P(("groups", "seq"), ("head", "rep")),
            P(("head", "rep"), ("groups", "seq")),
            P(None, ("head", "rep"), None, None),
            P("seq", ("head", "rep"), None, None),
        ),
        out_specs=(
            P(("groups", "seq"), ("head", "rep")),
            P(("groups", "seq"), ("head", "rep"), None, None),
            P(("groups", "seq"), ("head", "rep"), None, None),
        ),
        check_vma=False,
    )
```

```python
import functools
import math

import jax
import jax.numpy as jnp
from jax import lax
from jax.experimental import pallas as pl
from jax.experimental.pallas import tpu as pltpu
from jax.sharding import PartitionSpec as P


WIN = 512
TILE = 256

momentum_keep = 0.9
epsilon = 1e-06
MASKED = -1e30
LOG2E = math.log2(math.e)
PARAMS = pltpu.CompilerParams(vmem_limit_bytes=24 * 2**20)
VMEM = pl.BlockSpec(memory_space=pltpu.VMEM)
NT = (((1,), (1,)), ((), ()))


def call(body, grid, in_specs, out_specs, out_shape, scratch=(), prefetch=0, flops=0, nbytes=0):
    return pl.pallas_call(
        body,
        out_shape=out_shape,
        grid_spec=pltpu.PrefetchScalarGridSpec(
            num_scalar_prefetch=prefetch,
            grid=grid,
            in_specs=in_specs,
            out_specs=out_specs,
            scratch_shapes=list(scratch),
        ),
        compiler_params=PARAMS,
        cost_estimate=pl.CostEstimate(flops=flops, bytes_accessed=nbytes, transcendentals=0),
    )


def far(x):
    return pltpu.with_memory_space_constraint(x, pltpu.HBM)


def sigmoid(x):
    return 0.5 * jnp.tanh(0.5 * x) + 0.5


def dot(a, b, dims=None):
    if dims is None:
        return jnp.dot(a, b, preferred_element_type=jnp.float32)
    return lax.dot_general(a, b, dims, preferred_element_type=jnp.float32)


def steps_of(heads, most=5):
    return next(n for n in range(min(heads, most), 0, -1) if heads % n == 0)


def grad_body(peers, group, chunk, z_ref, k_ref, v_ref, r_ref, w_ref, *refs):
    outs, total = refs[:peers], refs[peers]
    size = w_ref.shape[2]
    rows = k_ref.shape[0]
    own = outs[0].shape[2]
    first = pl.program_id(0) * group
    tasks = [(g, c) for g in range(group) for c in range(0, rows, chunk)]
    turned = {}

    def products(g, c):
        if g not in turned:
            flipped = [jnp.transpose(w_ref[g, m]) for m in range(3)]
            turned[g] = (jnp.concatenate(flipped[:2], axis=0), flipped[2])
        cols, span = slice(g * size, (g + 1) * size), slice(c, c + chunk)
        inner = dot(turned[g][0], k_ref[span, cols], NT)
        return inner, dot(turned[g][1], v_ref[span, cols], NT)

    def finish(g, c, inner, back, sums):
        cols, span = slice(g * size, (g + 1) * size), slice(c, c + chunk)
        rate = r_ref[pl.ds(first + g, 1), span]
        gate, up = inner[:size], inner[size:]
        back = back * rate
        sig = sigmoid(gate)
        silu = gate * sig
        hidden = (silu * (up * rate)).astype(jnp.bfloat16)
        gate_grad = (back * up * (sig + silu * (1.0 - sig))).astype(jnp.bfloat16)
        up_grad = (back * silu).astype(jnp.bfloat16)
        found = [
            dot(jnp.concatenate([gate_grad, up_grad], axis=0), k_ref[span, cols]),
            dot(hidden, v_ref[span, cols]),
        ]
        sums = found if sums is None else [a + b for a, b in zip(sums, found)]
        if c + chunk < rows:
            return sums
        total[g % 2, 0] = jnp.transpose(sums[0][:size])
        total[g % 2, 1] = jnp.transpose(sums[0][size:])
        total[g % 2, 2] = jnp.transpose(sums[1])
        for m in range(peers):
            row = pl.multiple_of((z_ref[0] ^ m) * own, own)
            outs[m][g] = total[g % 2, :, pl.ds(row, own), :].astype(outs[m].dtype)
        return None

    sums = None
    ready = products(*tasks[0])
    for i, task in enumerate(tasks):
        following = products(*tasks[i + 1]) if i + 1 < len(tasks) else None
        sums = finish(*task, *ready, sums)
        ready = following


def partial_grads(z, keys, values, rates, weights, peers, kinds):
    rows = keys.shape[0]
    heads, _, size, _ = weights.shape
    own = size // peers
    group = steps_of(heads)
    column = pl.BlockSpec((rows, group * size), lambda h, z: (0, h))
    return call(
        functools.partial(grad_body, peers, group, min(rows, 256)),
        (heads // group,),
        [
            column,
            column,
            pl.BlockSpec((heads, rows), lambda h, z: (0, 0)),
            pl.BlockSpec((group, 3, size, size), lambda h, z: (h, 0, 0, 0)),
        ],
        [pl.BlockSpec((group, 3, own, size), lambda h, z: (h, 0, 0, 0))] * peers,
        [jax.ShapeDtypeStruct((heads, 3, own, size), kind) for kind in kinds],
        [pltpu.VMEM((2, 3, size, size), jnp.float32)],
        1,
        12 * rows * heads * size * size,
        4 * rows * heads * size,
    )(z, far(keys), far(values), far(rates), far(weights))


def update_body(count, z_ref, w_ref, m_ref, *refs):
    terms, w_out, m_out = refs[:count], refs[count], refs[count + 1]
    for g in range(w_ref.shape[0]):
        new = momentum_keep * m_ref[g]
        for term in terms:
            new = new + term[g].astype(jnp.float32)
        before = w_ref[g].astype(jnp.float32)
        moved = before + new
        ratio = jnp.sqrt(
            (jnp.mean(before * before, axis=-1, keepdims=True) + epsilon)
            / (jnp.mean(moved * moved, axis=-1, keepdims=True) + epsilon)
        )
        m_out[g] = new
        w_out[g] = (moved * ratio).astype(w_out.dtype)


def updated(z, weights, momentum, terms):
    shape = momentum.shape
    whole = pl.BlockSpec(shape, lambda i, z: (0, 0, 0, 0))
    count = momentum.size
    return call(
        functools.partial(update_body, len(terms)),
        (1,),
        [pl.BlockSpec(shape, lambda i, z: (0, 0, z[0], 0)), whole] + [VMEM] * len(terms),
        [VMEM, whole],
        [jax.ShapeDtypeStruct(shape, jnp.bfloat16), jax.ShapeDtypeStruct(shape, jnp.float32)],
        (),
        1,
        20 * count,
        16 * count,
    )(z, weights, momentum, *terms)


def attend(tasks, s_ref):
    def scores(i):
        query, segments, _ = tasks[i]
        query = query()
        top = None
        for j, (key, _, mask) in enumerate(segments):
            score = dot(key(), query, NT)
            if mask is not None:
                score = jnp.where(mask, score, MASKED)
            s_ref[i % 2, j * TILE : (j + 1) * TILE, :] = score
            most = jnp.max(score.reshape(TILE // 8, 8, TILE), axis=0)
            top = most if top is None else jnp.maximum(top, most)
        return jnp.max(top, axis=0, keepdims=True)

    def weigh(i, top):
        _, segments, emit = tasks[i]
        factor = segments[0][0]().shape[1] ** (-0.5)
        out = total = None
        for j, (_, value, _) in enumerate(segments):
            score = s_ref[i % 2, j * TILE : (j + 1) * TILE, :]
            weight = jnp.exp2((score - top) * (factor * LOG2E))
            part = jnp.sum(weight.reshape(TILE // 8, 8, TILE), axis=0)
            product = dot(value(), weight.astype(jnp.bfloat16))
            total = part if total is None else total + part
            out = product if out is None else out + product
        total = jnp.sum(total, axis=0, keepdims=True)
        emit(out * (1.0 / total), top * factor + jnp.log(total))

    top = scores(0)
    for i in range(len(tasks)):
        following = scores(i + 1) if i + 1 < len(tasks) else None
        weigh(i, top)
        top = following


def masks():
    row = lax.broadcasted_iota(jnp.int32, (TILE, TILE), 0)
    col = lax.broadcasted_iota(jnp.int32, (TILE, TILE), 1)
    return row <= col, row > col


def spans(ref, t, cols):
    return lambda: ref[t * TILE : (t + 1) * TILE, cols]


def turned(memo, ref, t, cols, key):
    def load():
        if (key, t) not in memo:
            memo[key, t] = jnp.transpose(ref[t * TILE : (t + 1) * TILE, cols])
        return memo[key, t]

    return load


def put(o_ref, t, cols):
    def emit(out, level):
        o_ref[t * TILE : (t + 1) * TILE, cols] = jnp.transpose(out).astype(o_ref.dtype)

    return emit


SCORES = (WIN // TILE + 1) * TILE


def later_body(group, q_ref, k_ref, v_ref, *refs):
    o_ref, s_ref = refs[-2:]
    size = q_ref.shape[1] // group
    causal, late = masks()
    depth = WIN // TILE
    tasks = []
    for g in range(group):
        cols = slice(g * size, (g + 1) * size)
        memo = {}
        for t in range(depth, q_ref.shape[0] // TILE):
            found = [
                (
                    spans(k_ref, j, cols),
                    turned(memo, v_ref, j, cols, 0),
                    causal if j == t else late if j == t - depth else None,
                )
                for j in range(t - depth, t + 1)
            ]
            tasks.append((spans(q_ref, t, cols), found, put(o_ref, t - depth, cols)))
    attend(tasks, s_ref)


def later_blocks(queries, keys, values, size, step, group, partly):
    rows, width = queries.shape
    column = pl.BlockSpec((rows, group * size), lambda h: (0, step))
    more = [] if partly is None else [partly]
    return pl.pallas_call(
        functools.partial(later_body, group),
        name="later",
        out_shape=jax.ShapeDtypeStruct((rows - WIN, width), jnp.bfloat16),
        grid_spec=pltpu.PrefetchScalarGridSpec(
            num_scalar_prefetch=0,
            grid=(1,),
            in_specs=[column] * 3 + [pl.BlockSpec(memory_space=pl.ANY)] * len(more),
            out_specs=pl.BlockSpec((rows - WIN, group * size), lambda h: (0, step)),
            scratch_shapes=[pltpu.VMEM((2, SCORES, TILE), jnp.float32)],
        ),
        compiler_params=PARAMS,
        input_output_aliases={3: 0} if more else {},
        cost_estimate=pl.CostEstimate(
            flops=6 * (rows - WIN) * WIN * size * group,
            bytes_accessed=8 * rows * size * group,
            transcendentals=0,
        ),
    )(*[x if more else far(x) for x in (queries, keys, values)], *more)


def carried_body(group, z_ref, q_ref, k_ref, v_ref, p_ref, o_ref, s_ref):
    size = q_ref.shape[1] // group
    causal, late = masks()
    depth = WIN // TILE
    there = jnp.broadcast_to(z_ref[0] > 0, causal.shape)
    tasks = []
    for g in range(group):
        cols = slice(g * size, (g + 1) * size)
        memo = {}
        for t in range(depth):
            found = [
                (spans(p_ref.at[0], j, cols), turned(memo, p_ref.at[1], j, cols, 1), late & there if j == t else there)
                for j in range(t, depth)
            ]
            found += [
                (spans(k_ref, j, cols), turned(memo, v_ref, j, cols, 0), causal if j == t else None)
                for j in range(t + 1)
            ]
            tasks.append((spans(q_ref, t, cols), found, put(o_ref, t, cols)))
    attend(tasks, s_ref)


def carried_block(z, queries, keys, values, carried, size):
    heads = carried.shape[2] // size
    group = heads
    width = queries.shape[1]
    column = pl.BlockSpec((WIN, group * size), lambda h, z: (0, h))
    return call(
        functools.partial(carried_body, group),
        (heads // group,),
        [column] * 3 + [VMEM],
        column,
        jax.ShapeDtypeStruct((WIN, width), jnp.bfloat16),
        [pltpu.VMEM((2, SCORES, TILE), jnp.float32)],
        1,
        6 * WIN * WIN * size * heads,
        10 * WIN * size * heads,
    )(z, queries, keys, values, carried)


EXTRA = 8
KEPT = 3
EARLY = 5


def put_partial(o_ref, g, t, size):
    def emit(out, level):
        span = slice(t * TILE, (t + 1) * TILE)
        o_ref[g, :size, span] = out.astype(o_ref.dtype)
        rest, parts = level, []
        for _ in range(3):
            term = rest.astype(jnp.bfloat16).astype(jnp.float32)
            parts.append(term)
            rest = rest - term
        parts.append(jnp.zeros((EXTRA - 3, TILE), jnp.float32))
        o_ref[g, size:, span] = jnp.concatenate(parts, axis=0).astype(o_ref.dtype)

    return emit


def next_part_body(group, skip, q_ref, k_ref, v_ref, o_ref, s_ref):
    size = k_ref.shape[1] // group
    start = skip + pl.program_id(0) * group if q_ref.shape[1] > group * size else 0
    _, late = masks()
    depth = WIN // TILE
    tasks = []
    for g in range(group):
        cols = slice(g * size, (g + 1) * size)
        memo = {}
        for t in range(depth):
            found = [
                (spans(k_ref, j, cols), turned(memo, v_ref, j, cols, 0), late if j == t else None)
                for j in range(t, depth)
            ]
            lanes = pl.ds(pl.multiple_of((start + g) * size, size), size)
            tasks.append((spans(q_ref, t, lanes), found, put_partial(o_ref, g, t, size)))
    attend(tasks, s_ref)


def next_part(asked, keys, values, skip, first, heads, size):
    block = keys.shape[0] // WIN - 1
    group = math.gcd(heads, first)
    column = pl.BlockSpec((WIN, group * size), lambda h: (block, h + first // group))
    return call(
        functools.partial(next_part_body, group, skip),
        (heads // group,),
        [VMEM, column, column],
        pl.BlockSpec((group, size + EXTRA, WIN), lambda h: (h, 0, 0)),
        jax.ShapeDtypeStruct((heads, size + EXTRA, WIN), jnp.bfloat16),
        [pltpu.VMEM((2, WIN, TILE), jnp.float32)],
        0,
        4 * WIN * WIN * size * heads,
        8 * WIN * size * heads,
    )(asked, keys, values)


def joined_body(group, z_ref, q_ref, k_ref, v_ref, p_ref, _, o_ref, s_ref):
    size = q_ref.shape[1] // group
    causal, _ = masks()
    depth = WIN // TILE
    step = pl.program_id(0) * group

    def join(g, t, cols):
        def emit(out, level):
            span = slice(t * TILE, (t + 1) * TILE)
            terms = p_ref[step + g, size:, span].astype(jnp.float32)
            other = terms[0:1] + (terms[1:2] + terms[2:3])
            share = jnp.where(z_ref[0] > 0, jax.nn.sigmoid(other - level), 0.0)
            out = out + share * (p_ref[step + g, :size, span].astype(jnp.float32) - out)
            o_ref[span, cols] = jnp.transpose(out).astype(o_ref.dtype)

        return emit

    tasks = []
    for g in range(group):
        cols = slice(g * size, (g + 1) * size)
        memo = {}
        for t in range(depth):
            found = [
                (spans(k_ref, j, cols), turned(memo, v_ref, j, cols, 0), causal if j == t else None)
                for j in range(t + 1)
            ]
            tasks.append((spans(q_ref, t, cols), found, join(g, t, cols)))
    attend(tasks, s_ref)


def joined_block(z, queries, keys, values, given, partly, first, size):
    heads = given.shape[0]
    group = math.gcd(heads, first)
    column = pl.BlockSpec((WIN, group * size), lambda h, z: (0, h + first // group))
    return pl.pallas_call(
        functools.partial(joined_body, group),
        name="joined",
        out_shape=jax.ShapeDtypeStruct(partly.shape, partly.dtype),
        grid_spec=pltpu.PrefetchScalarGridSpec(
            num_scalar_prefetch=1,
            grid=(heads // group,),
            in_specs=[
                column,
                column,
                column,
                VMEM,
                pl.BlockSpec(memory_space=pl.ANY),
            ],
            out_specs=column,
            scratch_shapes=[pltpu.VMEM((2, WIN, TILE), jnp.float32)],
        ),
        compiler_params=PARAMS,
        input_output_aliases={5: 0},
        cost_estimate=pl.CostEstimate(
            flops=4 * WIN * WIN * size * heads, bytes_accessed=10 * WIN * size * heads, transcendentals=0
        ),
    )(z, queries, keys, values, given, partly)


def own_part_body(group, q_ref, k_ref, v_ref, o_ref, s_ref):
    size = q_ref.shape[1] // group
    causal, _ = masks()
    tasks = []
    for g in range(group):
        cols = slice(g * size, (g + 1) * size)
        memo = {}
        for t in range(WIN // TILE):
            found = [
                (spans(k_ref, j, cols), turned(memo, v_ref, j, cols, 0), causal if j == t else None)
                for j in range(t + 1)
            ]
            tasks.append((spans(q_ref, t, cols), found, put_partial(o_ref, g, t, size)))
    attend(tasks, s_ref)


def own_part(queries, keys, values, first, heads, size):
    group = math.gcd(heads, first)
    column = pl.BlockSpec((WIN, group * size), lambda h: (0, h + first // group))
    return call(
        functools.partial(own_part_body, group),
        (heads // group,),
        [column] * 3,
        pl.BlockSpec((group, size + EXTRA, WIN), lambda h: (h, 0, 0)),
        jax.ShapeDtypeStruct((heads, size + EXTRA, WIN), jnp.bfloat16),
        [pltpu.VMEM((2, WIN, TILE), jnp.float32)],
        0,
        4 * WIN * WIN * size * heads,
        8 * WIN * size * heads,
    )(queries, keys, values)


def level_of(ref, head, size):
    terms = ref[head, size:, :].astype(jnp.float32)
    return terms[0:1] + (terms[1:2] + terms[2:3])


def merged_body(group, z_ref, a_ref, b_ref, base_ref, o_ref):
    size = base_ref.shape[1] // group
    step = pl.program_id(0) * group
    for g in range(group):
        cols = slice(g * size, (g + 1) * size)
        share = jax.nn.sigmoid(level_of(b_ref, step + g, size) - level_of(a_ref, step + g, size))
        share = jnp.where(z_ref[0] > 0, share, 0.0)
        own = a_ref[step + g, :size, :].astype(jnp.float32)
        out = own + share * (b_ref[step + g, :size, :].astype(jnp.float32) - own)
        out = jnp.transpose(out) + base_ref[:, cols].astype(jnp.float32)
        o_ref[:, cols] = out.astype(o_ref.dtype)


def merged(z, own, given, mixed, first, size):
    heads = own.shape[0]
    group = math.gcd(heads, first)
    column = pl.BlockSpec((WIN, group * size), lambda h, z: (0, h + first // group))
    return pl.pallas_call(
        functools.partial(merged_body, group),
        name="merged",
        out_shape=jax.ShapeDtypeStruct(mixed.shape, mixed.dtype),
        grid_spec=pltpu.PrefetchScalarGridSpec(
            num_scalar_prefetch=1,
            grid=(heads // group,),
            in_specs=[VMEM, VMEM, column],
            out_specs=column,
        ),
        compiler_params=PARAMS,
        input_output_aliases={3: 0},
        cost_estimate=pl.CostEstimate(
            flops=8 * WIN * size * heads, bytes_accessed=8 * WIN * size * heads, transcendentals=0
        ),
    )(z, own, given, mixed)


def final_body(peers, group, start, limit, z_ref, q_ref, first_ref, later_ref, *refs):
    blocks, o_ref, whole = refs[:peers], refs[-2], refs[-1]
    size = q_ref.shape[1] // group
    own = blocks[0].shape[2]
    for m in range(peers):
        row = pl.multiple_of((z_ref[0] ^ m) * own, own)
        base = start if m + 1 < peers else 0
        whole[:, :, pl.ds(row, own), :] = blocks[m][base : base + group].astype(whole.dtype)
    tasks = [(g, c) for g in range(group) for c in range(0, q_ref.shape[0], WIN)]

    def products(g, c):
        query = q_ref[c : c + WIN, g * size : (g + 1) * size]
        both = jnp.concatenate([whole[g, 0], whole[g, 1]], axis=1).astype(jnp.bfloat16)
        return dot(query, both)

    def finish(g, c, inner):
        cols = slice(g * size, (g + 1) * size)
        gate, up = inner[:, :size], inner[:, size:]
        hidden = (gate * sigmoid(gate) * up).astype(jnp.bfloat16)
        fast = dot(hidden, whole[g, 2].astype(jnp.bfloat16), NT)
        if c or start + g < limit:
            kept = later_ref[c - WIN : c, cols] if c else first_ref[:, cols]
            fast = fast + kept.astype(jnp.float32)
        o_ref[c : c + WIN, cols] = fast.astype(o_ref.dtype)

    ready = products(*tasks[0])
    for i, task in enumerate(tasks):
        following = products(*tasks[i + 1]) if i + 1 < len(tasks) else None
        finish(*task, ready)
        ready = following


def final(z, queries, first, later, blocks, size, step, group, limit, partly):
    rows, width = queries.shape
    peers, own = len(blocks), blocks[0].shape[2]
    kind = jnp.bfloat16 if own % 16 == 0 else jnp.float32
    more = [] if partly is None else [partly]
    return pl.pallas_call(
        functools.partial(final_body, peers, group, step * group, limit),
        name="final",
        out_shape=jax.ShapeDtypeStruct((rows, width), jnp.bfloat16),
        grid_spec=pltpu.PrefetchScalarGridSpec(
            num_scalar_prefetch=1,
            grid=(1,),
            in_specs=[
                pl.BlockSpec((rows, group * size), lambda h, z: (0, step)),
                pl.BlockSpec((WIN, group * size), lambda h, z: (0, step)),
                pl.BlockSpec((rows - WIN, group * size), lambda h, z: (0, step)),
            ]
            + [VMEM] * peers
            + [pl.BlockSpec(memory_space=pl.ANY)] * len(more),
            out_specs=pl.BlockSpec((rows, group * size), lambda h, z: (0, step)),
            scratch_shapes=[pltpu.VMEM((group, 3, size, size), kind)],
        ),
        compiler_params=PARAMS,
        input_output_aliases={4 + peers: 0} if more else {},
        cost_estimate=pl.CostEstimate(
            flops=6 * rows * group * size * size,
            bytes_accessed=6 * rows * group * size,
            transcendentals=0,
        ),
    )(z, queries, first, later, *blocks, *more)


def pack_body(first, q_ref, k_ref, v_ref, ask_ref, carry_ref, sems):
    cut = carry_ref.shape[2]
    tail = pl.ds(q_ref.shape[0] - WIN, WIN)
    copies = [
        (k_ref.at[tail, pl.ds(0, cut)], carry_ref.at[0]),
        (v_ref.at[tail, pl.ds(0, cut)], carry_ref.at[1]),
        (q_ref.at[pl.ds(0, WIN), pl.ds(first, ask_ref.shape[1])], ask_ref),
    ]
    copies = [pltpu.make_async_copy(*c, sems.at[i]) for i, c in enumerate(copies)]
    for copy in copies:
        copy.start()
    for copy in copies:
        copy.wait()


def packed(queries, keys, values, cut, asked):
    here = pl.BlockSpec(memory_space=pltpu.HBM)
    shapes = [(WIN, asked[1]), (2, WIN, cut)]
    return call(
        functools.partial(pack_body, asked[0]),
        (),
        [here] * 3,
        [VMEM] * 2,
        [jax.ShapeDtypeStruct(shape, queries.dtype) for shape in shapes],
        [pltpu.SemaphoreType.DMA((3,))],
        0,
        0,
        4 * WIN * (2 * cut + asked[1]),
    )(far(queries), far(keys), far(values))


def moved_by(value, by):
    peers = lax.axis_size("seq")
    pairs = [(i, i + by) for i in range(peers) if 0 <= i + by < peers]
    return lax.ppermute(value, "seq", pairs)


def swapped(value, mask):
    return lax.ppermute(value, "seq", [(i, i ^ mask) for i in range(lax.axis_size("seq"))])


def kept_of(heads):
    return max(1, heads * KEPT // 10)


def shards(queries, keys, values, rates, fast_weights, momentum):
    heads = rates.shape[0]
    size = fast_weights.shape[0]
    peers = lax.axis_size("seq")
    kept = kept_of(heads)
    z = lax.axis_index("seq").astype(jnp.int32).reshape(1)
    early = max(1, heads * EARLY // 10)
    late = kept + early
    lead = early // 2
    groups = [(kept, lead, 0, 0), (kept + lead, early - lead, 0, lead), (late, heads - late, 1, 0)]

    asked, carried = packed(queries, keys, values, kept * size, (kept * size, early * size))
    asked = [moved_by(asked, -1)]
    asked.append(moved_by(queries[:WIN, late * size :], -1))
    carried = moved_by(carried, 1)

    weights = jnp.transpose(fast_weights, (1, 2, 0, 3))
    own_momentum = jnp.transpose(momentum, (1, 2, 0, 3))
    kinds = [jnp.bfloat16 if m % 2 else jnp.float32 for m in range(peers)]
    sums = [[block] for block in partial_grads(z, keys, values, rates, weights, peers, kinds)]

    step = 1
    while step < peers:
        for m in reversed(range(peers)):
            if m % (2 * step) == step:
                terms = sums[m]
                block = functools.reduce(jnp.add, [t.astype(jnp.float32) for t in terms])
                sums[m - step].append(swapped(block.astype(jnp.bfloat16), step))
        step *= 2

    group = steps_of(heads)
    later = None
    for part in range(heads // group):
        later = later_blocks(queries, keys, values, size, part, group, later)
    given = []
    for place, count, source, skip in groups:
        part = next_part(asked[source], keys, values, skip, place, count, size)
        given.append(moved_by(part, 1))
    first = carried_block(z, queries, keys, values, carried, size)
    for i, (place, _, _, _) in enumerate(groups[:-1]):
        first = joined_block(z, queries, keys, values, given[i], first, place, size)

    new_rows, new_momentum = updated(z, weights, own_momentum, sums[0])
    blocks = {0: new_rows}
    step = peers // 2
    while step:
        for m in sorted(blocks):
            if m + step < peers - 1:
                blocks[m + step] = swapped(blocks[m], step)
        step //= 2

    mixed = None
    for part in range(heads // group):
        last = swapped(blocks[peers - 2][part * group : (part + 1) * group], 1)
        parts = [blocks[m] for m in range(peers - 1)] + [last]
        mixed = final(z, queries, first, later, parts, size, part, group, groups[-1][0], mixed)
    place, count, _, _ = groups[-1]
    own_last = own_part(queries, keys, values, place, count, size)
    mixed = merged(z, own_last, given[-1], mixed, place, size)
    return (mixed, jnp.transpose(new_rows, (2, 0, 1, 3)), jnp.transpose(new_momentum, (2, 0, 1, 3)))


def solution(mesh):
    return jax.shard_map(
        shards,
        mesh=mesh,
        in_specs=(
            P(("groups", "seq"), ("head", "rep")),
            P(("groups", "seq"), ("head", "rep")),
            P(("groups", "seq"), ("head", "rep")),
            P(("head", "rep"), ("groups", "seq")),
            P(None, ("head", "rep"), None, None),
            P("seq", ("head", "rep"), None, None),
        ),
        out_specs=(
            P(("groups", "seq"), ("head", "rep")),
            P(("groups", "seq"), ("head", "rep"), None, None),
            P(("groups", "seq"), ("head", "rep"), None, None),
        ),
        check_vma=False,
    )
```
